512 devices in a mesh: seq: 64 (over z, y), head: 8 (over x, core).
Axes of the slice: x: 4, y: 4, z: 16, core: 2. Of those that a mesh axis runs over, the one named last changes fastest.
Arguments:
- queries: bfloat16 [16384, 4096], P('seq', 'head'), may hold values from -0.29882812 to 0.29882812
- keys: bfloat16 [16384, 4096], P('seq', 'head'), may hold values from -0.29882812 to 0.29882812
- values: bfloat16 [16384, 4096], P('seq', 'head'), may hold values from -0.59765625 to 0.59765625
- out_grad: bfloat16 [16384, 4096], P('seq', 'head'), may hold values from -6 to 6
- doc_lengths: int32 [32], replicated, may hold values from 1 to 1024, 16384 in all
Outputs:
- query_grad: bfloat16 [16384, 4096], P(('seq', 'head'))
- key_grad: bfloat16 [16384, 4096], P(('seq', 'head'))
- value_grad: bfloat16 [16384, 4096], P(('seq', 'head'))
The draws below stay inside these ranges and needn't reach their ends.
Inputs may be any that keep to these rules, and one draw needn't show every extreme that they name: `doc_lengths`: the lengths sum to 16384 and the largest equals 1024.
All inputs are finite; a program needn't handle non-finite values.
Results may differ from the reference program's by a relative error of at most 0.0033.
Values may be sent and summed in bfloat16 or wider, within the bound.
A program may use at most 128 MiB of HBM per device.

```python
import math
import jax
import jax.numpy as jnp
import numpy as np
from jax import lax

HEADS = 32
HEAD_DIM = 128
D = 4096
TOK_DEV = 256
TOKENS = 16384
MOST = 1024
NDOCS = 32


def levels(own_key, shape, cuts, low, largest):
    loudness = 1.0
    for dim, blocks in cuts:
        draws = jax.random.uniform(jax.random.fold_in(jax.random.fold_in(own_key, 6), dim), (blocks,), jnp.float32, low / len(cuts), largest / len(cuts))
        loudness = loudness * jnp.repeat(jnp.exp(draws), shape[dim] // blocks).reshape((-1,) + (1,) * (len(shape) - 1 - dim))
    return loudness


def profile(number_of, total, reach, slope):
    weights = [(1 << 20) // math.isqrt(rank ** slope) + 1 for rank in range(2, number_of + 1)]
    spare, holding = total - reach - (number_of - 1), [1] * (number_of - 1)
    while spare > 0:
        movable = [i for i in range(number_of - 1) if holding[i] < reach]
        mass, budget = sum([weights[i] for i in movable]), spare
        for i in movable:
            more = min(reach - holding[i], max(1, budget * weights[i] // mass), spare)
            holding[i] = holding[i] + more
            spare = spare - more
    return np.array([reach] + holding)


def ragged(own_key, count, total, most, lean):
    if count == 2:
        one = jax.random.randint(own_key, (), max(1, total - most), min(most, total - 1) + 1)
        return jnp.stack([one, total - one])
    tallies = jnp.asarray(profile(count, total, most, lean), jnp.int32)
    pairs = (count - 1) // 2
    donor, receiver = tallies[1:1 + 2 * pairs:2], tallies[2:2 + 2 * pairs:2]
    margin = jnp.minimum(donor - 1, most - receiver)
    moved = jax.random.randint(jax.random.fold_in(own_key, 1), (pairs,), 0, 1 << 20) % (margin + 1)
    tallies = tallies.at[1:1 + 2 * pairs:2].set(donor - moved).at[2:2 + 2 * pairs:2].set(receiver + moved)
    return tallies[jax.random.permutation(jax.random.fold_in(own_key, 2), count)]


def bell_draw(stream_key, dims, width, bound, cuts=(), kind=jnp.bfloat16):
    gain = levels(stream_key, dims, cuts, -0.22, 0.18) if cuts else 1.0
    entries = jax.random.normal(stream_key, dims, jnp.float32) * width * gain
    return jnp.minimum(jnp.maximum(entries, -bound), bound).astype(kind)


def setup_inputs(seed: int = 0) -> dict:
    seeds = jax.random.split(jax.random.key(seed), 6)
    queries = bell_draw(seeds[0], (TOKENS, D), 0.05, 0.29882812, ((0, 64), (1, 8)))
    keys = bell_draw(seeds[1], (TOKENS, D), 0.05, 0.29882812, ((0, 64), (1, 8)))
    values = bell_draw(seeds[2], (TOKENS, D), 0.1, 0.59765625, ((0, 64), (1, 8)))
    out_grad = bell_draw(seeds[3], (TOKENS, D), 1.0, 6.0, ((0, 64), (1, 8)))
    doc_lengths = ragged(seeds[4], NDOCS, TOKENS, MOST, 2).astype(jnp.int32)
    return dict(queries=queries, keys=keys, values=values, out_grad=out_grad, doc_lengths=doc_lengths)


def doc_tables(doc_lengths):
    starts = jnp.cumsum(doc_lengths) - doc_lengths
    position = jnp.arange(TOKENS, dtype=jnp.int32)
    before = starts[None, :] <= position[:, None]
    doc_index = jnp.sum(before.astype(jnp.int32), axis=1) - 1
    doc_begin = jnp.max(jnp.where(before, starts[None, :], 0), axis=1)
    return doc_index, doc_begin


def block_grads(item):
    query_block, key_block, value_block, grad_block, doc_block, first_rows, last_rows, state_in, grad_in = item
    query_f = query_block.astype(jnp.float32)
    key_f = key_block.astype(jnp.float32)
    value_f = value_block.astype(jnp.float32)
    grad_f = grad_block.astype(jnp.float32)
    order = jnp.arange(TOK_DEV, dtype=jnp.int32)
    pair_mask = (doc_block[:, None] == doc_block[None, :]) & (order[:, None] >= order[None, :])
    score_qk = jnp.einsum("thd,shd->hts", query_f, key_f)
    weight_qk = jnp.where(pair_mask[None], score_qk, 0.0).astype(jnp.bfloat16).astype(jnp.float32)
    score_gv = jnp.einsum("the,she->hts", grad_f, value_f)
    weight_gv = jnp.where(pair_mask[None], score_gv, 0.0).astype(jnp.bfloat16).astype(jnp.float32)
    high = lax.Precision.HIGHEST
    carry_query = jnp.einsum("hde,the->thd", state_in, grad_f, precision=high)
    carry_key = jnp.einsum("hde,she->shd", grad_in, value_f, precision=high)
    carry_value = jnp.einsum("hde,shd->she", grad_in, key_f, precision=high)
    query_out = jnp.einsum("hts,shd->thd", weight_gv, key_f) + jnp.where(first_rows[:, None, None], carry_query, 0.0)
    key_out = jnp.einsum("hts,thd->shd", weight_gv, query_f) + jnp.where(last_rows[:, None, None], carry_key, 0.0)
    value_out = jnp.einsum("hts,the->she", weight_qk, grad_f) + jnp.where(last_rows[:, None, None], carry_value, 0.0)
    return (query_out.reshape(TOK_DEV, D).astype(jnp.bfloat16),
            key_out.reshape(TOK_DEV, D).astype(jnp.bfloat16),
            value_out.reshape(TOK_DEV, D).astype(jnp.bfloat16))


def reference(queries, keys, values, out_grad, doc_lengths):
    blocks = TOKENS // TOK_DEV
    doc_index, doc_begin = doc_tables(doc_lengths)
    doc_blocks = doc_index.reshape(blocks, TOK_DEV)
    begin_blocks = doc_begin.reshape(blocks, TOK_DEV)
    block_start = jnp.arange(blocks, dtype=jnp.int32) * TOK_DEV
    first_rows = begin_blocks < block_start[:, None]
    last_rows = doc_blocks == doc_blocks[:, TOK_DEV - 1:TOK_DEV]
    has_start = jnp.any(begin_blocks >= block_start[:, None], axis=1).astype(jnp.float32)
    shape4 = (blocks, TOK_DEV, HEADS, HEAD_DIM)
    query_b = queries.reshape(shape4)
    key_b = keys.reshape(shape4)
    value_b = values.reshape(shape4)
    grad_b = out_grad.reshape(shape4)
    empty = jnp.zeros((HEADS, HEAD_DIM, HEAD_DIM), jnp.float32)

    def forward_step(state, item):
        key_block, value_block, rows, started = item
        picked = jnp.where(rows[:, None, None], key_block.astype(jnp.float32), 0.0)
        tail_state = jnp.einsum("lhd,lhe->hde", picked, value_block.astype(jnp.float32))
        return (1.0 - started) * state + tail_state, state

    def backward_step(state, item):
        query_block, grad_block, rows, started = item
        picked = jnp.where(rows[:, None, None], query_block.astype(jnp.float32), 0.0)
        head_state = jnp.einsum("lhd,lhe->hde", picked, grad_block.astype(jnp.float32))
        return head_state + (1.0 - started) * state, state

    _, states_in = lax.scan(forward_step, empty, (key_b, value_b, last_rows, has_start))
    _, grads_in = lax.scan(backward_step, empty, (query_b, grad_b, first_rows, has_start), reverse=True)
    query_grad, key_grad, value_grad = lax.map(block_grads, (query_b, key_b, value_b, grad_b, doc_blocks, first_rows, last_rows, states_in, grads_in))
    return (query_grad.reshape(TOKENS, D), key_grad.reshape(TOKENS, D), value_grad.reshape(TOKENS, D))
```

```python
import jax
import jax.numpy as jnp
from jax import lax
from jax.sharding import PartitionSpec as P

HEAD_DIM = 128
REACH = 4


def make_shards(blocks):
    def shards(queries, keys, values, out_grad, doc_lengths):
        rows_dev = queries.shape[0]
        width = queries.shape[1]
        head_count = width // HEAD_DIM
        block = lax.axis_index("seq")
        shard_begin = block * rows_dev
        ends = jnp.cumsum(doc_lengths)
        starts = ends - doc_lengths
        order = jnp.arange(rows_dev, dtype=jnp.int32)
        position = shard_begin + order
        before = starts[None, :] <= position[:, None]
        doc_index = jnp.sum(before.astype(jnp.int32), axis=1) - 1
        doc_begin = jnp.max(jnp.where(before, starts[None, :], 0), axis=1)
        first_begin = doc_begin[0]
        last_end = jnp.sum(jnp.where(doc_index[rows_dev - 1] == jnp.arange(doc_lengths.shape[0]), ends, 0))
        first_rows = doc_begin < shard_begin
        last_rows = doc_index == doc_index[rows_dev - 1]
        query_heads = queries.reshape(rows_dev, head_count, HEAD_DIM)
        key_heads = keys.reshape(rows_dev, head_count, HEAD_DIM)
        value_heads = values.reshape(rows_dev, head_count, HEAD_DIM)
        grad_heads = out_grad.reshape(rows_dev, head_count, HEAD_DIM)
        tail_keys = jnp.where(last_rows[:, None, None], key_heads, jnp.zeros_like(key_heads))
        tail_state = jnp.einsum(
            "lhd,lhe->hde", tail_keys, value_heads, preferred_element_type=jnp.float32
        ).astype(jnp.bfloat16)
        head_queries = jnp.where(first_rows[:, None, None], query_heads, jnp.zeros_like(query_heads))
        head_state = jnp.einsum(
            "lhd,lhe->hde", head_queries, grad_heads, preferred_element_type=jnp.float32
        ).astype(jnp.bfloat16)
        state_in = jnp.zeros((head_count, HEAD_DIM, HEAD_DIM), jnp.float32)
        grad_in = jnp.zeros((head_count, HEAD_DIM, HEAD_DIM), jnp.float32)
        for j in range(1, REACH + 1):
            came = lax.ppermute(tail_state, "seq", [(i, (i + j) % blocks) for i in range(blocks)])
            use = first_begin < rows_dev * (block - j + 1)
            state_in = state_in + jnp.where(use, came.astype(jnp.float32), 0.0)
            came = lax.ppermute(head_state, "seq", [(i, (i - j) % blocks) for i in range(blocks)])
            use = last_end > rows_dev * (block + j)
            grad_in = grad_in + jnp.where(use, came.astype(jnp.float32), 0.0)
        state_in = state_in.astype(jnp.bfloat16)
        grad_in = grad_in.astype(jnp.bfloat16)
        pair_mask = (doc_index[:, None] == doc_index[None, :]) & (order[:, None] >= order[None, :])
        score_qk = jnp.einsum(
            "thd,shd->hts", query_heads, key_heads, preferred_element_type=jnp.float32
        )
        weight_qk = jnp.where(pair_mask[None], score_qk, 0.0).astype(jnp.bfloat16)
        score_gv = jnp.einsum(
            "the,she->hts", grad_heads, value_heads, preferred_element_type=jnp.float32
        )
        weight_gv = jnp.where(pair_mask[None], score_gv, 0.0).astype(jnp.bfloat16)
        carry_query = jnp.einsum(
            "hde,the->thd", state_in, grad_heads, preferred_element_type=jnp.float32
        )
        query_local = jnp.einsum(
            "hts,shd->thd", weight_gv, key_heads, preferred_element_type=jnp.float32
        )
        query_out = (
            (query_local + jnp.where(first_rows[:, None, None], carry_query, 0.0))
            .reshape(rows_dev, width)
            .astype(jnp.bfloat16)
        )
        carry_key = jnp.einsum("hde,she->shd", grad_in, value_heads, preferred_element_type=jnp.float32)
        carry_value = jnp.einsum("hde,shd->she", grad_in, key_heads, preferred_element_type=jnp.float32)
        key_local = jnp.einsum(
            "hts,thd->shd", weight_gv, query_heads, preferred_element_type=jnp.float32
        )
        value_local = jnp.einsum(
            "hts,the->she", weight_qk, grad_heads, preferred_element_type=jnp.float32
        )
        key_out = (
            (key_local + jnp.where(last_rows[:, None, None], carry_key, 0.0))
            .reshape(rows_dev, width)
            .astype(jnp.bfloat16)
        )
        value_out = (
            (value_local + jnp.where(last_rows[:, None, None], carry_value, 0.0))
            .reshape(rows_dev, width)
            .astype(jnp.bfloat16)
        )
        return (
            lax.all_to_all(query_out, "head", split_axis=0, concat_axis=1, tiled=True),
            lax.all_to_all(key_out, "head", split_axis=0, concat_axis=1, tiled=True),
            lax.all_to_all(value_out, "head", split_axis=0, concat_axis=1, tiled=True),
        )

    return shards


def solution(mesh):
    return jax.shard_map(
        make_shards(mesh.shape["seq"]),
        mesh=mesh,
        in_specs=(P("seq", "head"), P("seq", "head"), P("seq", "head"), P("seq", "head"), P()),
        out_specs=(P(("seq", "head"), None), P(("seq", "head"), None), P(("seq", "head"), None)),
        check_vma=False,
    )
```

```python
import functools

import jax
import jax.numpy as jnp
from jax import lax
from jax.experimental import pallas as pl
from jax.experimental.pallas import tpu as pltpu
from jax.sharding import PartitionSpec as P

HEAD_DIM = 128
MESH = pl.DeviceIdType.MESH
F32 = jnp.float32
BF16 = jnp.bfloat16

NN = (((1,), (0,)), ((), ()))
NT = (((1,), (1,)), ((), ()))
TN = (((0,), (0,)), ((), ()))


def mm(a, b, dims):
    return lax.dot_general(a, b, dims, preferred_element_type=F32)


def kernel(
    blocks, groups,
    q_hbm, k_hbm, v_hbm, g_hbm, len_ref,
    out_ref,
    q_ref, k_ref, v_ref, g_ref, local, own, first, pair, made,
    in_sem, state_send, state_recv, out_send, out_recv, own_sem,
):
    rows, width = q_ref.shape
    heads = width // HEAD_DIM
    rows_out = rows // groups
    b = lax.axis_index("seq")
    h = lax.axis_index("head")

    loads = [
        pltpu.make_async_copy(src, dst, in_sem.at[i])
        for i, (src, dst) in enumerate(((k_hbm, k_ref), (v_hbm, v_ref), (q_hbm, q_ref), (g_hbm, g_ref)))
    ]
    for load in loads:
        load.start()

    shifts = (1, 3, -1, -3)
    neighbours = {s: lax.rem(b + s + blocks, blocks) for s in shifts}
    order = sorted(range(1, groups), key=lambda k: -min(k // 2, (groups - k) // 2))
    peers = {k: lax.rem(h + k, groups) for k in order}

    barrier = pltpu.get_barrier_semaphore()
    for s in shifts:
        pl.semaphore_signal(barrier, inc=1, device_id={"seq": neighbours[s]}, device_id_type=MESH)
    for k in order:
        pl.semaphore_signal(barrier, inc=1, device_id={"head": peers[k]}, device_id_type=MESH)

    docs = len_ref.shape[1]
    begin_block = (b * rows).astype(F32)
    lengths = jnp.broadcast_to(len_ref[...].astype(F32), (docs, docs))
    down = lax.broadcasted_iota(jnp.int32, (docs, docs), 0)
    across = lax.broadcasted_iota(jnp.int32, (docs, docs), 1)
    length_col = jnp.sum(jnp.where(down == across, lengths, 0.0), axis=1, keepdims=True)
    ends = jnp.sum(jnp.where(down <= across, length_col, 0.0), axis=0, keepdims=True)
    starts = ends - lengths[:1]
    far = 1e9
    place = lax.broadcasted_iota(jnp.int32, (rows, docs), 0).astype(F32) + begin_block
    starts_all = jnp.broadcast_to(starts, (rows, docs))
    ends_all = jnp.broadcast_to(ends, (rows, docs))
    doc_begin = jnp.max(jnp.where(starts_all <= place, starts_all, 0.0), axis=1, keepdims=True)
    doc_end = jnp.min(jnp.where(ends_all > place, ends_all, far), axis=1, keepdims=True)
    last_place = begin_block + (rows - 1)
    begin_first = jnp.max(jnp.where(starts <= begin_block, starts, 0.0), axis=1, keepdims=True)
    begin_last = jnp.max(jnp.where(starts <= last_place, starts, 0.0), axis=1, keepdims=True)
    end_last = jnp.min(jnp.where(ends > last_place, ends, far), axis=1, keepdims=True)
    through = (begin_last < begin_block).astype(F32)
    far_before = (begin_first < begin_block - 2 * rows).astype(F32)
    far_after = (end_last > begin_block + 3 * rows).astype(F32)
    first_rows = jnp.broadcast_to((doc_begin < begin_block).astype(F32), (rows, HEAD_DIM)).astype(BF16)
    last_rows = jnp.broadcast_to((doc_end > last_place).astype(F32), (rows, HEAD_DIM)).astype(BF16)
    row = lax.broadcasted_iota(jnp.int32, (rows, rows), 0).astype(F32)
    col = lax.broadcasted_iota(jnp.int32, (rows, rows), 1).astype(F32)
    pair[0] = ((col >= doc_begin - begin_block) & (col <= row)).astype(F32).astype(BF16)
    pair[1] = ((col < doc_end - begin_block) & (col >= row)).astype(F32).astype(BF16)

    def cols(i):
        return pl.ds(i * HEAD_DIM, HEAD_DIM)

    def state_copy(i, way, kind):
        s = ((1, 1, 3), (-1, -1, -3))[way][kind]
        return pltpu.make_async_remote_copy(
            src_ref=first.at[way, min(kind, 1), i],
            dst_ref=first.at[way, 2 + kind, i],
            send_sem=state_send.at[way, kind, i],
            recv_sem=state_recv.at[way, kind, i],
            device_id={"seq": neighbours[s]},
            device_id_type=MESH,
        )

    def out_copy(i, k):
        return pltpu.make_async_remote_copy(
            src_ref=made.at[i, :, pl.ds(pl.multiple_of(peers[k] * rows_out, rows_out), rows_out), :],
            dst_ref=out_ref.at[:, :, pl.ds(pl.multiple_of(h * width + i * HEAD_DIM, HEAD_DIM), HEAD_DIM)],
            send_sem=out_send.at[k, i],
            recv_sem=out_recv.at[k, i],
            device_id={"head": peers[k]},
            device_id_type=MESH,
        )

    def own_copy(i):
        return pltpu.make_async_copy(
            made.at[i, :, pl.ds(pl.multiple_of(h * rows_out, rows_out), rows_out), :],
            out_ref.at[:, :, pl.ds(pl.multiple_of(h * width + i * HEAD_DIM, HEAD_DIM), HEAD_DIM)],
            own_sem.at[i],
        )

    def states(i):
        tail = mm(v_ref[:, cols(i)], k_ref[:, cols(i)] * last_rows, TN)
        own[0, i] = tail
        first[0, 0, i] = tail.astype(BF16)
        head = mm(q_ref[:, cols(i)], g_ref[:, cols(i)] * first_rows, TN)
        own[1, i] = head
        first[1, 0, i] = head.astype(BF16)

    def pass_on(i):
        for way in range(2):
            state_copy(i, way, 0).wait_recv()
            both = own[way, i] + through * first[way, 2, i].astype(F32)
            first[way, 1, i] = both.astype(BF16)
            state_copy(i, way, 1).start()
            state_copy(i, way, 2).start()

    def inner(i):
        q, k, v, g = (ref[:, cols(i)] for ref in (q_ref, k_ref, v_ref, g_ref))
        weight = mm(g, v, NT).astype(BF16) * pair[0]
        local[0, i] = mm(weight, k, NN)
        weight = mm(v, g, NT).astype(BF16) * pair[1]
        local[1, i] = mm(weight, q, NN)
        weight = mm(k, q, NT).astype(BF16) * pair[1]
        local[2, i] = mm(weight, g, NN)

    def whole(way, i, reach):
        state_copy(i, way, 1).wait_recv()
        state_copy(i, way, 2).wait_recv()
        total = first[way, 3, i].astype(F32) + reach * first[way, 4, i].astype(F32)
        high = total.astype(BF16)
        return high, (total - high.astype(F32)).astype(BF16)

    def finish(i):
        high, low = whole(0, i, far_before)
        g = g_ref[:, cols(i)] * first_rows
        made[i, 0] = (local[0, i] + (mm(g, high, NN) + mm(g, low, NN))).astype(BF16)
        high, low = whole(1, i, far_after)
        v = v_ref[:, cols(i)] * last_rows
        made[i, 1] = (local[1, i] + (mm(v, high, NT) + mm(v, low, NT))).astype(BF16)
        k = k_ref[:, cols(i)] * last_rows
        made[i, 2] = (local[2, i] + (mm(k, high, NN) + mm(k, low, NN))).astype(BF16)
        for peer in order:
            out_copy(i, peer).start()
        own_copy(i).start()

    for load in loads:
        load.wait()
    states(0)
    pl.semaphore_wait(barrier, len(shifts) + len(order))
    for i in range(heads):
        if i:
            states(i)
        for way in range(2):
            state_copy(i, way, 0).start()
    half = max(heads // 2, 1)
    for i in range(half):
        inner(i)
    for i in range(half):
        pass_on(i)
    for i in range(half, heads):
        pass_on(i)
        inner(i)
    for i in range(heads):
        finish(i)
    for i in range(heads):
        own_copy(i).wait()
        for way in range(2):
            for kind in range(3):
                state_copy(i, way, kind).wait_send()
        for k in order:
            out_copy(i, k).wait()


def make_shards(blocks, groups):
    def shards(queries, keys, values, out_grad, doc_lengths):
        rows, width = queries.shape
        heads = width // HEAD_DIM
        rows_out = rows // groups
        out = pl.pallas_call(
            functools.partial(kernel, blocks, groups),
            out_shape=jax.ShapeDtypeStruct((3, rows_out, width * groups), BF16),
            in_specs=[pl.BlockSpec(memory_space=pl.ANY)] * 4 + [pl.BlockSpec(memory_space=pltpu.VMEM)],
            out_specs=pl.BlockSpec(memory_space=pltpu.VMEM),
            scratch_shapes=[pltpu.VMEM((rows, width), BF16)] * 4
            + [
                pltpu.VMEM((3, heads, rows, HEAD_DIM), F32),
                pltpu.VMEM((2, heads, HEAD_DIM, HEAD_DIM), F32),
                pltpu.VMEM((2, 5, heads, HEAD_DIM, HEAD_DIM), BF16),
                pltpu.VMEM((2, rows, rows), BF16),
                pltpu.VMEM((heads, 3, rows, HEAD_DIM), BF16),
                pltpu.SemaphoreType.DMA((4,)),
                pltpu.SemaphoreType.DMA((2, 3, heads)),
                pltpu.SemaphoreType.DMA((2, 3, heads)),
                pltpu.SemaphoreType.DMA((groups, heads)),
                pltpu.SemaphoreType.DMA((groups, heads)),
                pltpu.SemaphoreType.DMA((heads,)),
            ],
            compiler_params=pltpu.CompilerParams(collective_id=0, has_side_effects=True),
        )(queries, keys, values, out_grad, doc_lengths.reshape(1, -1))
        return out[0], out[1], out[2]

    return shards


def solution(mesh):
    return jax.shard_map(
        make_shards(mesh.shape["seq"], mesh.shape["head"]),
        mesh=mesh,
        in_specs=(P("seq", "head"), P("seq", "head"), P("seq", "head"), P("seq", "head"), P()),
        out_specs=(P(("seq", "head"), None), P(("seq", "head"), None), P(("seq", "head"), None)),
        check_vma=False,
    )
```

```python
import functools

import jax
import jax.numpy as jnp
from jax import lax
from jax.experimental import pallas as pl
from jax.experimental.pallas import tpu as pltpu
from jax.sharding import PartitionSpec as P

HEAD_DIM = 128
MESH = pl.DeviceIdType.MESH
F32 = jnp.float32
BF16 = jnp.bfloat16

NN = (((1,), (0,)), ((), ()))
NT = (((1,), (1,)), ((), ()))
TN = (((0,), (0,)), ((), ()))


def mm(a, b, dims):
    return lax.dot_general(a, b, dims, preferred_element_type=F32)


def kernel(
    blocks, groups,
    q_hbm, k_hbm, v_hbm, g_hbm, len_ref,
    out_ref,
    q_ref, k_ref, v_ref, g_ref, local, own, first, pair, made,
    in_sem, state_send, state_recv, out_send, out_recv, own_sem,
):
    rows, width = q_ref.shape
    heads = width // HEAD_DIM
    rows_out = rows // groups
    b = lax.axis_index("seq")
    h = lax.axis_index("head")

    loads = [
        pltpu.make_async_copy(src, dst, in_sem.at[i])
        for i, (src, dst) in enumerate(((k_hbm, k_ref), (v_hbm, v_ref), (q_hbm, q_ref), (g_hbm, g_ref)))
    ]
    for load in loads:
        load.start()

    shifts = (1, 3, -1, -3)
    inside = {s: b + s < blocks if s > 0 else b + s >= 0 for s in shifts}
    order = sorted(range(1, groups), key=lambda k: -min(k // 2, (groups - k) // 2))
    peers = {k: lax.rem(h + k, groups) for k in order}

    barrier = pltpu.get_barrier_semaphore()
    for s in shifts:
        @pl.when(inside[s])
        def _():
            pl.semaphore_signal(barrier, inc=1, device_id={"seq": b + s}, device_id_type=MESH)
    for k in order:
        pl.semaphore_signal(barrier, inc=1, device_id={"head": peers[k]}, device_id_type=MESH)

    docs = len_ref.shape[1]
    begin_block = (b * rows).astype(F32)
    lengths = jnp.broadcast_to(len_ref[...].astype(F32), (docs, docs))
    down = lax.broadcasted_iota(jnp.int32, (docs, docs), 0)
    across = lax.broadcasted_iota(jnp.int32, (docs, docs), 1)
    length_col = jnp.sum(jnp.where(down == across, lengths, 0.0), axis=1, keepdims=True)
    ends = jnp.sum(jnp.where(down <= across, length_col, 0.0), axis=0, keepdims=True)
    starts = ends - lengths[:1]
    far = 1e9
    place = lax.broadcasted_iota(jnp.int32, (rows, docs), 0).astype(F32) + begin_block
    starts_all = jnp.broadcast_to(starts, (rows, docs))
    ends_all = jnp.broadcast_to(ends, (rows, docs))
    doc_begin = jnp.max(jnp.where(starts_all <= place, starts_all, 0.0), axis=1, keepdims=True)
    doc_end = jnp.min(jnp.where(ends_all > place, ends_all, far), axis=1, keepdims=True)
    last_place = begin_block + (rows - 1)
    begin_first = jnp.max(jnp.where(starts <= begin_block, starts, 0.0), axis=1, keepdims=True)
    begin_last = jnp.max(jnp.where(starts <= last_place, starts, 0.0), axis=1, keepdims=True)
    end_last = jnp.min(jnp.where(ends > last_place, ends, far), axis=1, keepdims=True)
    through = (begin_last < begin_block).astype(F32)
    far_before = (begin_first < begin_block - 2 * rows).astype(F32)
    far_after = (end_last > begin_block + 3 * rows).astype(F32)
    first_rows = jnp.broadcast_to((doc_begin < begin_block).astype(F32), (rows, HEAD_DIM)).astype(BF16)
    last_rows = jnp.broadcast_to((doc_end > last_place).astype(F32), (rows, HEAD_DIM)).astype(BF16)

    def pairs():
        row = lax.broadcasted_iota(jnp.int32, (rows, rows), 0).astype(F32)
        col = lax.broadcasted_iota(jnp.int32, (rows, rows), 1).astype(F32)
        pair[0] = ((col >= doc_begin - begin_block) & (col <= row)).astype(F32).astype(BF16)
        pair[1] = ((col < doc_end - begin_block) & (col >= row)).astype(F32).astype(BF16)

    for way in range(2):
        for kind in range(3):
            @pl.when(jnp.logical_not(inside[((-1, -1, -3), (1, 1, 3))[way][kind]]))
            def _():
                first[way, 2 + kind] = jnp.zeros(first.shape[2:], BF16)

    def cols(i):
        return pl.ds(i * HEAD_DIM, HEAD_DIM)

    def state_copy(i, way, kind):
        s = ((1, 1, 3), (-1, -1, -3))[way][kind]
        return pltpu.make_async_remote_copy(
            src_ref=first.at[way, min(kind, 1), i],
            dst_ref=first.at[way, 2 + kind, i],
            send_sem=state_send.at[way, kind, i],
            recv_sem=state_recv.at[way, kind, i],
            device_id={"seq": b + s},
            device_id_type=MESH,
        )

    def to(way, kind):
        return inside[((1, 1, 3), (-1, -1, -3))[way][kind]]

    def came(way, kind):
        return inside[((-1, -1, -3), (1, 1, 3))[way][kind]]

    def out_copy(i, k):
        return pltpu.make_async_remote_copy(
            src_ref=made.at[i, :, pl.ds(pl.multiple_of(peers[k] * rows_out, rows_out), rows_out), :],
            dst_ref=out_ref.at[:, :, pl.ds(pl.multiple_of(h * width + i * HEAD_DIM, HEAD_DIM), HEAD_DIM)],
            send_sem=out_send.at[k, i],
            recv_sem=out_recv.at[k, i],
            device_id={"head": peers[k]},
            device_id_type=MESH,
        )

    def own_copy(i):
        return pltpu.make_async_copy(
            made.at[i, :, pl.ds(pl.multiple_of(h * rows_out, rows_out), rows_out), :],
            out_ref.at[:, :, pl.ds(pl.multiple_of(h * width + i * HEAD_DIM, HEAD_DIM), HEAD_DIM)],
            own_sem.at[i],
        )

    def states(i):
        tail = mm(v_ref[:, cols(i)], k_ref[:, cols(i)] * last_rows, TN)
        own[0, i] = tail
        first[0, 0, i] = tail.astype(BF16)
        head = mm(q_ref[:, cols(i)], g_ref[:, cols(i)] * first_rows, TN)
        own[1, i] = head
        first[1, 0, i] = head.astype(BF16)

    def send_own(i):
        for way in range(2):
            @pl.when(to(way, 0))
            def _():
                state_copy(i, way, 0).start()

    def pass_on(i):
        for way in range(2):
            @pl.when(came(way, 0))
            def _():
                state_copy(i, way, 0).wait_recv()
            both = own[way, i] + through * first[way, 2, i].astype(F32)
            first[way, 1, i] = both.astype(BF16)
            for kind in (1, 2):
                @pl.when(to(way, kind))
                def _():
                    state_copy(i, way, kind).start()

    def inner(i):
        q, k, v, g = (ref[:, cols(i)] for ref in (q_ref, k_ref, v_ref, g_ref))
        weight = mm(g, v, NT).astype(BF16) * pair[0]
        local[0, i] = mm(weight, k, NN)
        weight = mm(v, g, NT).astype(BF16) * pair[1]
        local[1, i] = mm(weight, q, NN)
        weight = mm(k, q, NT).astype(BF16) * pair[1]
        local[2, i] = mm(weight, g, NN)

    def arrive(i):
        for way in range(2):
            for kind in (1, 2):
                @pl.when(came(way, kind))
                def _():
                    state_copy(i, way, kind).wait_recv()

    def whole(way, i, reach):
        total = first[way, 3, i].astype(F32) + reach * first[way, 4, i].astype(F32)
        high = total.astype(BF16)
        return high, (total - high.astype(F32)).astype(BF16)

    def finish(i):
        arrive(i)
        high, low = whole(0, i, far_before)
        g = g_ref[:, cols(i)] * first_rows
        made[i, 0] = (local[0, i] + (mm(g, high, NN) + mm(g, low, NN))).astype(BF16)
        high, low = whole(1, i, far_after)
        v = v_ref[:, cols(i)] * last_rows
        made[i, 1] = (local[1, i] + (mm(v, high, NT) + mm(v, low, NT))).astype(BF16)
        k = k_ref[:, cols(i)] * last_rows
        made[i, 2] = (local[2, i] + (mm(k, high, NN) + mm(k, low, NN))).astype(BF16)
        for peer in order:
            out_copy(i, peer).start()
        own_copy(i).start()

    for load in loads:
        load.wait()
    states(0)
    pl.semaphore_wait(barrier, len(order) + sum(inside[s].astype(jnp.int32) for s in shifts))
    send_own(0)
    for i in range(1, heads):
        states(i)
        send_own(i)
    pairs()
    half = max(heads // 2, 1)
    for i in range(half):
        inner(i)
    for i in range(half):
        pass_on(i)
    for i in range(half, heads):
        pass_on(i)
        inner(i)
    for i in range(heads):
        finish(i)
    for i in range(heads):
        own_copy(i).wait()
        for way in range(2):
            for kind in range(3):
                @pl.when(to(way, kind))
                def _():
                    state_copy(i, way, kind).wait_send()
        for k in order:
            out_copy(i, k).wait()


def split(whole_ref, a_ref, b_ref, c_ref, sem):
    copies = [
        pltpu.make_async_copy(whole_ref.at[i], part, sem.at[i])
        for i, part in enumerate((a_ref, b_ref, c_ref))
    ]
    for copy in copies:
        copy.start()
    for copy in copies:
        copy.wait()


def make_shards(blocks, groups):
    def shards(queries, keys, values, out_grad, doc_lengths):
        rows, width = queries.shape
        heads = width // HEAD_DIM
        rows_out = rows // groups
        out = pl.pallas_call(
            functools.partial(kernel, blocks, groups),
            out_shape=pltpu.VMEM((3, rows_out, width * groups), BF16),
            in_specs=[pl.BlockSpec(memory_space=pltpu.HBM)] * 4 + [pl.BlockSpec(memory_space=pltpu.VMEM)],
            out_specs=pl.BlockSpec(memory_space=pltpu.VMEM),
            scratch_shapes=[pltpu.VMEM((rows, width), BF16)] * 4
            + [
                pltpu.VMEM((3, heads, rows, HEAD_DIM), F32),
                pltpu.VMEM((2, heads, HEAD_DIM, HEAD_DIM), F32),
                pltpu.VMEM((2, 5, heads, HEAD_DIM, HEAD_DIM), BF16),
                pltpu.VMEM((2, rows, rows), BF16),
                pltpu.VMEM((heads, 3, rows, HEAD_DIM), BF16),
                pltpu.SemaphoreType.DMA((4,)),
                pltpu.SemaphoreType.DMA((2, 3, heads)),
                pltpu.SemaphoreType.DMA((2, 3, heads)),
                pltpu.SemaphoreType.DMA((groups, heads)),
                pltpu.SemaphoreType.DMA((groups, heads)),
                pltpu.SemaphoreType.DMA((heads,)),
            ],
            compiler_params=pltpu.CompilerParams(
                collective_id=0, has_side_effects=True
            ),
        )(queries, keys, values, out_grad, doc_lengths.reshape(1, -1))
        part = jax.ShapeDtypeStruct((rows_out, width * groups), BF16)
        return pl.pallas_call(
            split,
            out_shape=(part, part, part),
            in_specs=[pl.BlockSpec(memory_space=pltpu.VMEM)],
            out_specs=(pl.BlockSpec(memory_space=pl.ANY),) * 3,
            scratch_shapes=[pltpu.SemaphoreType.DMA((3,))],
            compiler_params=pltpu.CompilerParams(vmem_limit_bytes=8 << 20),
        )(out)

    return shards


def solution(mesh):
    return jax.shard_map(
        make_shards(mesh.shape["seq"], mesh.shape["head"]),
        mesh=mesh,
        in_specs=(P("seq", "head"), P("seq", "head"), P("seq", "head"), P("seq", "head"), P()),
        out_specs=(P(("seq", "head"), None), P(("seq", "head"), None), P(("seq", "head"), None)),
        check_vma=False,
    )
```

```python
import functools

import jax
import jax.numpy as jnp
from jax import lax
from jax.experimental import pallas as pl
from jax.experimental.pallas import tpu as pltpu
from jax.sharding import PartitionSpec as P

HEAD_DIM = 128
MESH = pl.DeviceIdType.MESH
F32 = jnp.float32
BF16 = jnp.bfloat16

NN = (((1,), (0,)), ((), ()))
NT = (((1,), (1,)), ((), ()))
TN = (((0,), (0,)), ((), ()))


def mm(a, b, dims):
    return lax.dot_general(a, b, dims, preferred_element_type=F32)


def kernel(
    blocks, groups,
    q_hbm, k_hbm, v_hbm, g_hbm, len_hbm,
    out_ref,
    q_ref, k_ref, v_ref, g_ref, local, own, first, pair, made,
    len_ref, table_sem, in_sem, state_send, state_recv, out_send, out_recv, own_sem,
):
    rows, width = q_ref.shape
    heads = width // HEAD_DIM
    rows_out = rows // groups
    b = lax.axis_index("seq")
    h = lax.axis_index("head")

    def cols(i):
        return pl.ds(i * HEAD_DIM, HEAD_DIM)

    table_load = pltpu.make_async_copy(len_hbm, len_ref, table_sem)
    loads = [
        [
            pltpu.make_async_copy(src.at[:, cols(i)], dst.at[:, cols(i)], in_sem.at[n, i])
            for n, (src, dst) in enumerate(((k_hbm, k_ref), (v_hbm, v_ref), (q_hbm, q_ref), (g_hbm, g_ref)))
        ]
        for i in range(heads)
    ]
    table_load.start()
    for load in loads[0]:
        load.start()

    shifts = (1, 3, -1, -3)
    inside = {s: b + s < blocks if s > 0 else b + s >= 0 for s in shifts}
    order = sorted(range(1, groups), key=lambda k: -min(k // 2, (groups - k) // 2))
    peers = {k: lax.rem(h + k, groups) for k in order}

    barrier = pltpu.get_barrier_semaphore()
    for s in shifts:
        @pl.when(inside[s])
        def _():
            pl.semaphore_signal(barrier, inc=1, device_id={"seq": b + s}, device_id_type=MESH)
    for k in order:
        pl.semaphore_signal(barrier, inc=1, device_id={"head": peers[k]}, device_id_type=MESH)

    for load in sum(loads[1:], []):
        load.start()
    table_load.wait()

    docs = len_ref.shape[1]
    begin_block = (b * rows).astype(F32)
    lengths = jnp.broadcast_to(len_ref[...].astype(F32), (docs, docs))
    down = lax.broadcasted_iota(jnp.int32, (docs, docs), 0)
    across = lax.broadcasted_iota(jnp.int32, (docs, docs), 1)
    length_col = jnp.sum(jnp.where(down == across, lengths, 0.0), axis=1, keepdims=True)
    ends = jnp.sum(jnp.where(down <= across, length_col, 0.0), axis=0, keepdims=True)
    starts = ends - lengths[:1]
    far = 1e9
    place = lax.broadcasted_iota(jnp.int32, (rows, docs), 0).astype(F32) + begin_block
    starts_all = jnp.broadcast_to(starts, (rows, docs))
    ends_all = jnp.broadcast_to(ends, (rows, docs))
    doc_begin = jnp.max(jnp.where(starts_all <= place, starts_all, 0.0), axis=1, keepdims=True)
    doc_end = jnp.min(jnp.where(ends_all > place, ends_all, far), axis=1, keepdims=True)
    last_place = begin_block + (rows - 1)
    begin_first = jnp.max(jnp.where(starts <= begin_block, starts, 0.0), axis=1, keepdims=True)
    begin_last = jnp.max(jnp.where(starts <= last_place, starts, 0.0), axis=1, keepdims=True)
    end_last = jnp.min(jnp.where(ends > last_place, ends, far), axis=1, keepdims=True)
    through = (begin_last < begin_block).astype(F32)
    far_before = (begin_first < begin_block - 2 * rows).astype(F32)
    far_after = (end_last > begin_block + 3 * rows).astype(F32)
    first_rows = jnp.broadcast_to((doc_begin < begin_block).astype(F32), (rows, HEAD_DIM)).astype(BF16)
    last_rows = jnp.broadcast_to((doc_end > last_place).astype(F32), (rows, HEAD_DIM)).astype(BF16)

    def pairs():
        row = lax.broadcasted_iota(jnp.int32, (rows, rows), 0).astype(F32)
        col = lax.broadcasted_iota(jnp.int32, (rows, rows), 1).astype(F32)
        pair[0] = ((col >= doc_begin - begin_block) & (col <= row)).astype(F32).astype(BF16)
        pair[1] = ((col < doc_end - begin_block) & (col >= row)).astype(F32).astype(BF16)

    for way in range(2):
        for kind in range(3):
            @pl.when(jnp.logical_not(inside[((-1, -1, -3), (1, 1, 3))[way][kind]]))
            def _():
                first[way, 2 + kind] = jnp.zeros(first.shape[2:], BF16)

    def state_copy(i, way, kind):
        s = ((1, 1, 3), (-1, -1, -3))[way][kind]
        return pltpu.make_async_remote_copy(
            src_ref=first.at[way, min(kind, 1), i],
            dst_ref=first.at[way, 2 + kind, i],
            send_sem=state_send.at[way, kind, i],
            recv_sem=state_recv.at[way, kind, i],
            device_id={"seq": b + s},
            device_id_type=MESH,
        )

    def to(way, kind):
        return inside[((1, 1, 3), (-1, -1, -3))[way][kind]]

    def came(way, kind):
        return inside[((-1, -1, -3), (1, 1, 3))[way][kind]]

    def out_copy(i, k):
        return pltpu.make_async_remote_copy(
            src_ref=made.at[i, :, pl.ds(pl.multiple_of(peers[k] * rows_out, rows_out), rows_out), :],
            dst_ref=out_ref.at[:, :, pl.ds(pl.multiple_of(h * width + i * HEAD_DIM, HEAD_DIM), HEAD_DIM)],
            send_sem=out_send.at[k, i],
            recv_sem=out_recv.at[k, i],
            device_id={"head": peers[k]},
            device_id_type=MESH,
        )

    def own_copy(i):
        return pltpu.make_async_copy(
            made.at[i, :, pl.ds(pl.multiple_of(h * rows_out, rows_out), rows_out), :],
            out_ref.at[:, :, pl.ds(pl.multiple_of(h * width + i * HEAD_DIM, HEAD_DIM), HEAD_DIM)],
            own_sem.at[i],
        )

    def states(i):
        tail = mm(v_ref[:, cols(i)], k_ref[:, cols(i)] * last_rows, TN)
        own[0, i] = tail
        first[0, 0, i] = tail.astype(BF16)
        head = mm(q_ref[:, cols(i)], g_ref[:, cols(i)] * first_rows, TN)
        own[1, i] = head
        first[1, 0, i] = head.astype(BF16)

    def send_own(i):
        for way in range(2):
            @pl.when(to(way, 0))
            def _():
                state_copy(i, way, 0).start()

    def pass_on(i):
        for way in range(2):
            @pl.when(came(way, 0))
            def _():
                state_copy(i, way, 0).wait_recv()
            both = own[way, i] + through * first[way, 2, i].astype(F32)
            first[way, 1, i] = both.astype(BF16)
            for kind in (1, 2):
                @pl.when(to(way, kind))
                def _():
                    state_copy(i, way, kind).start()

    def inner(i):
        q, k, v, g = (ref[:, cols(i)] for ref in (q_ref, k_ref, v_ref, g_ref))
        weight = mm(g, v, NT).astype(BF16) * pair[0]
        local[0, i] = mm(weight, k, NN)
        weight = mm(v, g, NT).astype(BF16) * pair[1]
        local[1, i] = mm(weight, q, NN)
        weight = mm(k, q, NT).astype(BF16) * pair[1]
        local[2, i] = mm(weight, g, NN)

    def arrive(i):
        for way in range(2):
            for kind in (1, 2):
                @pl.when(came(way, kind))
                def _():
                    state_copy(i, way, kind).wait_recv()

    def whole(way, i, reach):
        total = first[way, 3, i].astype(F32) + reach * first[way, 4, i].astype(F32)
        high = total.astype(BF16)
        return high, (total - high.astype(F32)).astype(BF16)

    def finish(i):
        arrive(i)
        high, low = whole(0, i, far_before)
        g = g_ref[:, cols(i)] * first_rows
        made[i, 0] = (local[0, i] + (mm(g, high, NN) + mm(g, low, NN))).astype(BF16)
        high, low = whole(1, i, far_after)
        v = v_ref[:, cols(i)] * last_rows
        made[i, 1] = (local[1, i] + (mm(v, high, NT) + mm(v, low, NT))).astype(BF16)
        k = k_ref[:, cols(i)] * last_rows
        made[i, 2] = (local[2, i] + (mm(k, high, NN) + mm(k, low, NN))).astype(BF16)
        for peer in order:
            out_copy(i, peer).start()
        own_copy(i).start()

    for load in loads[0]:
        load.wait()
    states(0)
    pl.semaphore_wait(barrier, len(order) + sum(inside[s].astype(jnp.int32) for s in shifts))
    send_own(0)
    for i in range(1, heads):
        for load in loads[i]:
            load.wait()
        states(i)
        send_own(i)
    pairs()
    half = max(heads // 2, 1)
    for i in range(half):
        inner(i)
    for i in range(half):
        pass_on(i)
    for i in range(half, heads):
        pass_on(i)
        inner(i)
    for i in range(heads):
        finish(i)
    for i in range(heads):
        own_copy(i).wait()
        for way in range(2):
            for kind in range(3):
                @pl.when(to(way, kind))
                def _():
                    state_copy(i, way, kind).wait_send()
        for k in order:
            out_copy(i, k).wait()


def split(whole_ref, a_ref, b_ref, c_ref, sem):
    copies = [
        pltpu.make_async_copy(whole_ref.at[i], part, sem.at[i])
        for i, part in enumerate((a_ref, b_ref, c_ref))
    ]
    for copy in copies:
        copy.start()
    for copy in copies:
        copy.wait()


def make_shards(blocks, groups):
    def shards(queries, keys, values, out_grad, doc_lengths):
        rows, width = queries.shape
        heads = width // HEAD_DIM
        rows_out = rows // groups
        docs = doc_lengths.shape[0]
        out = pl.pallas_call(
            functools.partial(kernel, blocks, groups),
            out_shape=pltpu.VMEM((3, rows_out, width * groups), BF16),
            in_specs=[pl.BlockSpec(memory_space=pltpu.HBM)] * 5,
            out_specs=pl.BlockSpec(memory_space=pltpu.VMEM),
            scratch_shapes=[pltpu.VMEM((rows, width), BF16)] * 4
            + [
                pltpu.VMEM((3, heads, rows, HEAD_DIM), F32),
                pltpu.VMEM((2, heads, HEAD_DIM, HEAD_DIM), F32),
                pltpu.VMEM((2, 5, heads, HEAD_DIM, HEAD_DIM), BF16),
                pltpu.VMEM((2, rows, rows), BF16),
                pltpu.VMEM((heads, 3, rows, HEAD_DIM), BF16),
                pltpu.VMEM((1, docs), jnp.int32),
                pltpu.SemaphoreType.DMA,
                pltpu.SemaphoreType.DMA((4, heads)),
                pltpu.SemaphoreType.DMA((2, 3, heads)),
                pltpu.SemaphoreType.DMA((2, 3, heads)),
                pltpu.SemaphoreType.DMA((groups, heads)),
                pltpu.SemaphoreType.DMA((groups, heads)),
                pltpu.SemaphoreType.DMA((heads,)),
            ],
            compiler_params=pltpu.CompilerParams(
                collective_id=0, has_side_effects=True
            ),
        )(queries, keys, values, out_grad, doc_lengths.reshape(1, -1))
        part = jax.ShapeDtypeStruct((rows_out, width * groups), BF16)
        return pl.pallas_call(
            split,
            out_shape=(part, part, part),
            in_specs=[pl.BlockSpec(memory_space=pltpu.VMEM)],
            out_specs=(pl.BlockSpec(memory_space=pl.ANY),) * 3,
            scratch_shapes=[pltpu.SemaphoreType.DMA((3,))],
            compiler_params=pltpu.CompilerParams(vmem_limit_bytes=8 << 20),
        )(out)

    return shards


def solution(mesh):
    return jax.shard_map(
        make_shards(mesh.shape["seq"], mesh.shape["head"]),
        mesh=mesh,
        in_specs=(P("seq", "head"), P("seq", "head"), P("seq", "head"), P("seq", "head"), P()),
        out_specs=(P(("seq", "head"), None), P(("seq", "head"), None), P(("seq", "head"), None)),
        check_vma=False,
    )
```

```python
import functools

import jax
import jax.numpy as jnp
from jax import lax
from jax.experimental import pallas as pl
from jax.experimental.pallas import tpu as pltpu
from jax.sharding import PartitionSpec as P

HEAD_DIM = 128
MESH = pl.DeviceIdType.MESH
F32 = jnp.float32
BF16 = jnp.bfloat16

NN = (((1,), (0,)), ((), ()))
NT = (((1,), (1,)), ((), ()))
TN = (((0,), (0,)), ((), ()))


def mm(a, b, dims):
    return lax.dot_general(a, b, dims, preferred_element_type=F32)


def kernel(
    blocks, groups,
    q_hbm, k_hbm, v_hbm, g_hbm, len_hbm,
    out_ref,
    q_ref, k_ref, v_ref, g_ref, local, own, first, pair, made,
    len_ref, table_sem, in_sem, state_send, state_recv, out_send, out_recv, own_sem, late_sem,
):
    rows, width = q_ref.shape
    heads = width // HEAD_DIM
    rows_out = rows // groups
    b = lax.axis_index("seq")
    h = lax.axis_index("head")

    def cols(i):
        return pl.ds(i * HEAD_DIM, HEAD_DIM)

    table_load = pltpu.make_async_copy(len_hbm, len_ref, table_sem)
    loads = [
        [
            pltpu.make_async_copy(src.at[:, cols(i)], dst.at[:, cols(i)], in_sem.at[n, i])
            for n, (src, dst) in enumerate(((k_hbm, k_ref), (v_hbm, v_ref), (q_hbm, q_ref), (g_hbm, g_ref)))
        ]
        for i in range(heads)
    ]
    table_load.start()
    for load in loads[0]:
        load.start()

    late = (b == 0) & (h == 0)
    shifts = (1, 3, -1, -3)
    inside = {s: b + s < blocks if s > 0 else b + s >= 0 for s in shifts}
    order = sorted(range(1, groups), key=lambda k: -min(k // 2, (groups - k) // 2))
    peers = {k: lax.rem(h + k, groups) for k in order}

    barrier = pltpu.get_barrier_semaphore()
    for s in shifts:
        @pl.when(inside[s] & jnp.logical_not(late))
        def _():
            pl.semaphore_signal(barrier, inc=1, device_id={"seq": b + s}, device_id_type=MESH)
    for k in order:
        @pl.when(jnp.logical_not(late))
        def _():
            pl.semaphore_signal(barrier, inc=1, device_id={"head": peers[k]}, device_id_type=MESH)

    def late_seq(s):
        return (b + s == 0) & (h == 0)

    def late_head(k):
        return (b == 0) & (peers[k] == 0)

    def wait_late(there):
        @pl.when(there)
        def _():
            pl.semaphore_wait(late_sem, 1)

    def enter():
        waits = len(order) + sum(inside[s].astype(jnp.int32) for s in shifts)
        waits = waits - sum(late_seq(s).astype(jnp.int32) for s in shifts)
        waits = waits - sum(late_head(k).astype(jnp.int32) for k in order)
        pl.semaphore_wait(barrier, waits)
        for s in (1, 3):
            @pl.when(late)
            def _():
                pl.semaphore_signal(late_sem, inc=1, device_id={"seq": b + s}, device_id_type=MESH)
        for k in order:
            @pl.when(late)
            def _():
                pl.semaphore_signal(late_sem, inc=1, device_id={"head": peers[k]}, device_id_type=MESH)

    for load in sum(loads[1:], []):
        load.start()
    table_load.wait()

    docs = len_ref.shape[1]
    begin_block = (b * rows).astype(F32)
    lengths = jnp.broadcast_to(len_ref[...].astype(F32), (docs, docs))
    down = lax.broadcasted_iota(jnp.int32, (docs, docs), 0)
    across = lax.broadcasted_iota(jnp.int32, (docs, docs), 1)
    length_col = jnp.sum(jnp.where(down == across, lengths, 0.0), axis=1, keepdims=True)
    ends = jnp.sum(jnp.where(down <= across, length_col, 0.0), axis=0, keepdims=True)
    starts = ends - lengths[:1]
    far = 1e9
    place = lax.broadcasted_iota(jnp.int32, (rows, docs), 0).astype(F32) + begin_block
    starts_all = jnp.broadcast_to(starts, (rows, docs))
    ends_all = jnp.broadcast_to(ends, (rows, docs))
    doc_begin = jnp.max(jnp.where(starts_all <= place, starts_all, 0.0), axis=1, keepdims=True)
    doc_end = jnp.min(jnp.where(ends_all > place, ends_all, far), axis=1, keepdims=True)
    last_place = begin_block + (rows - 1)
    begin_first = jnp.max(jnp.where(starts <= begin_block, starts, 0.0), axis=1, keepdims=True)
    begin_last = jnp.max(jnp.where(starts <= last_place, starts, 0.0), axis=1, keepdims=True)
    end_last = jnp.min(jnp.where(ends > last_place, ends, far), axis=1, keepdims=True)
    through = (begin_last < begin_block).astype(F32)
    far_before = (begin_first < begin_block - 2 * rows).astype(F32)
    far_after = (end_last > begin_block + 3 * rows).astype(F32)
    first_rows = jnp.broadcast_to((doc_begin < begin_block).astype(F32), (rows, HEAD_DIM)).astype(BF16)
    last_rows = jnp.broadcast_to((doc_end > last_place).astype(F32), (rows, HEAD_DIM)).astype(BF16)

    def pairs():
        row = lax.broadcasted_iota(jnp.int32, (rows, rows), 0).astype(F32)
        col = lax.broadcasted_iota(jnp.int32, (rows, rows), 1).astype(F32)
        pair[0] = ((col >= doc_begin - begin_block) & (col <= row)).astype(F32).astype(BF16)
        pair[1] = ((col < doc_end - begin_block) & (col >= row)).astype(F32).astype(BF16)

    def to(way, kind):
        if kind == 0:
            return (b >= 2, b < blocks - 2)[1 - way]
        return inside[((1, 1, 3), (-1, -1, -3))[way][kind]]

    def came(way, kind):
        if kind == 0:
            return (b >= 1) & (b < blocks - 1)
        return inside[((-1, -1, -3), (1, 1, 3))[way][kind]]

    for way in range(2):
        for kind in range(3):
            @pl.when(jnp.logical_not(came(way, kind)))
            def _():
                first[way, 2 + kind] = jnp.zeros(first.shape[2:], BF16)

    def state_copy(i, way, kind):
        s = ((1, 1, 3), (-1, -1, -3))[way][kind]
        return pltpu.make_async_remote_copy(
            src_ref=first.at[way, min(kind, 1), i],
            dst_ref=first.at[way, 2 + kind, i],
            send_sem=state_send.at[way, kind, i],
            recv_sem=state_recv.at[way, kind, i],
            device_id={"seq": b + s},
            device_id_type=MESH,
        )

    def out_copy(i, part, k):
        return pltpu.make_async_remote_copy(
            src_ref=made.at[i, parts[part], pl.ds(pl.multiple_of(peers[k] * rows_out, rows_out), rows_out), :],
            dst_ref=out_ref.at[parts[part], :, pl.ds(pl.multiple_of(h * width + i * HEAD_DIM, HEAD_DIM), HEAD_DIM)],
            send_sem=out_send.at[part, k, i],
            recv_sem=out_recv.at[part, k, i],
            device_id={"head": peers[k]},
            device_id_type=MESH,
        )

    def own_copy(i, part):
        return pltpu.make_async_copy(
            made.at[i, parts[part], pl.ds(pl.multiple_of(h * rows_out, rows_out), rows_out), :],
            out_ref.at[parts[part], :, pl.ds(pl.multiple_of(h * width + i * HEAD_DIM, HEAD_DIM), HEAD_DIM)],
            own_sem.at[part, i],
        )

    parts = (pl.ds(0, 1), pl.ds(1, 2))

    def states(i):
        tail = mm(v_ref[:, cols(i)], k_ref[:, cols(i)] * last_rows, TN)
        own[0, i] = tail
        first[0, 0, i] = tail.astype(BF16)
        head = mm(q_ref[:, cols(i)], g_ref[:, cols(i)] * first_rows, TN)
        own[1, i] = head
        first[1, 0, i] = head.astype(BF16)

    def send_own(i):
        for way in range(2):
            @pl.when(to(way, 0))
            def _():
                state_copy(i, way, 0).start()

    def pass_on(i):
        for way in (1, 0):
            @pl.when(came(way, 0))
            def _():
                state_copy(i, way, 0).wait_recv()
            both = own[way, i] + through * first[way, 2, i].astype(F32)
            first[way, 1, i] = both.astype(BF16)
            for kind in (1, 2):
                if way == 1 and i == 0:
                    wait_late(late_seq((-1, -3)[kind - 1]))
                @pl.when(to(way, kind))
                def _():
                    state_copy(i, way, kind).start()

    def inner(i):
        q, k, v, g = (ref[:, cols(i)] for ref in (q_ref, k_ref, v_ref, g_ref))
        weight = mm(g, v, NT).astype(BF16) * pair[0]
        local[0, i] = mm(weight, k, NN)
        weight = mm(v, g, NT).astype(BF16) * pair[1]
        local[1, i] = mm(weight, q, NN)
        weight = mm(k, q, NT).astype(BF16) * pair[1]
        local[2, i] = mm(weight, g, NN)

    def arrive(i, way):
        for kind in (1, 2):
            @pl.when(came(way, kind))
            def _():
                state_copy(i, way, kind).wait_recv()

    def whole(way, i, reach):
        total = first[way, 3, i].astype(F32) + reach * first[way, 4, i].astype(F32)
        high = total.astype(BF16)
        return high, (total - high.astype(F32)).astype(BF16)

    def send_out(i, part):
        for k in order:
            if i == 0 and part == 1:
                wait_late(late_head(k))
            out_copy(i, part, k).start()
        own_copy(i, part).start()

    def finish(i):
        arrive(i, 1)
        high, low = whole(1, i, far_after)
        v = v_ref[:, cols(i)] * last_rows
        made[i, 1] = (local[1, i] + (mm(v, high, NT) + mm(v, low, NT))).astype(BF16)
        k = k_ref[:, cols(i)] * last_rows
        made[i, 2] = (local[2, i] + (mm(k, high, NN) + mm(k, low, NN))).astype(BF16)
        send_out(i, 1)
        arrive(i, 0)
        high, low = whole(0, i, far_before)
        g = g_ref[:, cols(i)] * first_rows
        made[i, 0] = (local[0, i] + (mm(g, high, NN) + mm(g, low, NN))).astype(BF16)
        send_out(i, 0)

    for load in loads[0]:
        load.wait()
    states(0)
    enter()
    send_own(0)
    for i in range(1, heads):
        for load in loads[i]:
            load.wait()
        states(i)
        send_own(i)
    pairs()
    half = max(heads // 2, 1)
    for i in range(half):
        inner(i)
    for i in range(half):
        pass_on(i)
    for i in range(half, heads):
        pass_on(i)
        inner(i)
    for i in range(heads):
        finish(i)
    for i in range(heads):
        for part in range(2):
            own_copy(i, part).wait()
            for k in order:
                out_copy(i, part, k).wait()
        for way in range(2):
            for kind in range(3):
                @pl.when(to(way, kind))
                def _():
                    state_copy(i, way, kind).wait_send()


def split(whole_ref, a_ref, b_ref, c_ref, sem):
    copies = [
        pltpu.make_async_copy(whole_ref.at[i], part, sem.at[i])
        for i, part in enumerate((a_ref, b_ref, c_ref))
    ]
    for copy in copies:
        copy.start()
    for copy in copies:
        copy.wait()


def make_shards(blocks, groups):
    def shards(queries, keys, values, out_grad, doc_lengths):
        rows, width = queries.shape
        heads = width // HEAD_DIM
        rows_out = rows // groups
        docs = doc_lengths.shape[0]
        out = pl.pallas_call(
            functools.partial(kernel, blocks, groups),
            out_shape=pltpu.VMEM((3, rows_out, width * groups), BF16),
            in_specs=[pl.BlockSpec(memory_space=pltpu.HBM)] * 5,
            out_specs=pl.BlockSpec(memory_space=pltpu.VMEM),
            scratch_shapes=[pltpu.VMEM((rows, width), BF16)] * 4
            + [
                pltpu.VMEM((3, heads, rows, HEAD_DIM), F32),
                pltpu.VMEM((2, heads, HEAD_DIM, HEAD_DIM), F32),
                pltpu.VMEM((2, 5, heads, HEAD_DIM, HEAD_DIM), BF16),
                pltpu.VMEM((2, rows, rows), BF16),
                pltpu.VMEM((heads, 3, rows, HEAD_DIM), BF16),
                pltpu.VMEM((1, docs), jnp.int32),
                pltpu.SemaphoreType.DMA,
                pltpu.SemaphoreType.DMA((4, heads)),
                pltpu.SemaphoreType.DMA((2, 3, heads)),
                pltpu.SemaphoreType.DMA((2, 3, heads)),
                pltpu.SemaphoreType.DMA((2, groups, heads)),
                pltpu.SemaphoreType.DMA((2, groups, heads)),
                pltpu.SemaphoreType.DMA((2, heads)),
                pltpu.SemaphoreType.REGULAR,
            ],
            compiler_params=pltpu.CompilerParams(
                collective_id=0, has_side_effects=True
            ),
        )(queries, keys, values, out_grad, doc_lengths.reshape(1, -1))
        part = jax.ShapeDtypeStruct((rows_out, width * groups), BF16)
        return pl.pallas_call(
            split,
            out_shape=(part, part, part),
            in_specs=[pl.BlockSpec(memory_space=pltpu.VMEM)],
            out_specs=(pl.BlockSpec(memory_space=pl.ANY),) * 3,
            scratch_shapes=[pltpu.SemaphoreType.DMA((3,))],
            compiler_params=pltpu.CompilerParams(vmem_limit_bytes=8 << 20),
        )(out)

    return shards


def solution(mesh):
    return jax.shard_map(
        make_shards(mesh.shape["seq"], mesh.shape["head"]),
        mesh=mesh,
        in_specs=(P("seq", "head"), P("seq", "head"), P("seq", "head"), P("seq", "head"), P()),
        out_specs=(P(("seq", "head"), None), P(("seq", "head"), None), P(("seq", "head"), None)),
        check_vma=False,
    )
```

```python
import functools

import jax
import jax.numpy as jnp
from jax import lax
from jax.experimental import pallas as pl
from jax.experimental.pallas import tpu as pltpu
from jax.sharding import PartitionSpec as P

HEAD_DIM = 128
MESH = pl.DeviceIdType.MESH
F32 = jnp.float32
BF16 = jnp.bfloat16

NN = (((1,), (0,)), ((), ()))
NT = (((1,), (1,)), ((), ()))
TN = (((0,), (0,)), ((), ()))


def mm(a, b, dims):
    return lax.dot_general(a, b, dims, preferred_element_type=F32)


def kernel(
    blocks, groups,
    q_hbm, k_hbm, v_hbm, g_hbm, len_hbm,
    out_ref,
    q_ref, k_ref, v_ref, g_ref, local, own, first, pair, made,
    len_ref, table_sem, in_sem, state_send, state_recv, out_send, out_recv, own_sem, late_sem,
):
    rows, width = q_ref.shape
    heads = width // HEAD_DIM
    rows_out = rows // groups
    b = lax.axis_index("seq")
    h = lax.axis_index("head")

    def cols(i):
        return pl.ds(i * HEAD_DIM, HEAD_DIM)

    table_load = pltpu.make_async_copy(len_hbm, len_ref, table_sem)
    loads = [
        [
            pltpu.make_async_copy(src.at[:, cols(i)], dst.at[:, cols(i)], in_sem.at[i])
            for src, dst in ((k_hbm, k_ref), (v_hbm, v_ref), (q_hbm, q_ref), (g_hbm, g_ref))
        ]
        for i in range(heads)
    ]

    def loaded(i):
        all_four = q_ref.at[:, pl.ds(0, 4 * HEAD_DIM)]
        pltpu.make_async_copy(all_four, all_four, in_sem.at[i]).wait()

    table_load.start()
    for load in loads[0]:
        load.start()

    late = (b == 0) & (h == 0)
    shifts = (1, 3, -1, -3)
    hops = (1, 1, 3)
    inside = {s: b + s < blocks if s > 0 else b + s >= 0 for s in shifts}
    order = sorted(range(1, groups), key=lambda k: -min(k // 2, (groups - k) // 2))
    peers = {k: lax.rem(h + k, groups) for k in order}

    barrier = pltpu.get_barrier_semaphore()

    @pl.when(jnp.logical_not(late))
    def _():
        for k in order:
            pl.semaphore_signal(barrier, inc=1, device_id={"head": peers[k]}, device_id_type=MESH)
        for s in shifts:
            @pl.when(inside[s])
            def _():
                pl.semaphore_signal(barrier, inc=1, device_id={"seq": b + s}, device_id_type=MESH)

    def late_seq(s):
        return (b + s == 0) & (h == 0)

    after_late = (h == 0) & (functools.reduce(jnp.logical_or, [b == s for s in shifts if s > 0]))
    beside_late = (b == 0) & (h != 0)

    def wait_late(there):
        @pl.when(there)
        def _():
            pl.semaphore_wait(late_sem, 1)

    def enter():
        waits = len(order) + sum(inside[s].astype(jnp.int32) for s in shifts)
        waits = waits - (after_late | beside_late).astype(jnp.int32)
        pl.semaphore_wait(barrier, waits)

        @pl.when(late)
        def _():
            for k in order:
                pl.semaphore_signal(late_sem, inc=1, device_id={"head": peers[k]}, device_id_type=MESH)
            for s in shifts:
                if s > 0:
                    pl.semaphore_signal(late_sem, inc=1, device_id={"seq": b + s}, device_id_type=MESH)

    for load in sum(loads[1:], []):
        load.start()
    table_load.wait()

    docs = len_ref.shape[1]
    begin_block = (b * rows).astype(F32)
    lengths = jnp.broadcast_to(len_ref[...].astype(F32), (docs, docs))
    down = lax.broadcasted_iota(jnp.int32, (docs, docs), 0)
    across = lax.broadcasted_iota(jnp.int32, (docs, docs), 1)
    length_col = jnp.sum(jnp.where(down == across, lengths, 0.0), axis=1, keepdims=True)
    ends = jnp.sum(jnp.where(down <= across, length_col, 0.0), axis=0, keepdims=True)
    starts = ends - lengths[:1]
    far = 1e9
    last_place = begin_block + (rows - 1)
    begin_first = jnp.max(jnp.where(starts <= begin_block, starts, 0.0), axis=1, keepdims=True)
    begin_last = jnp.max(jnp.where(starts <= last_place, starts, 0.0), axis=1, keepdims=True)
    begin_next = jnp.min(jnp.where(starts >= begin_block, starts, far), axis=1, keepdims=True)
    end_last = jnp.min(jnp.where(ends > last_place, ends, far), axis=1, keepdims=True)
    through = (begin_last < begin_block).astype(F32)
    reach = [
        (begin_first < begin_block - 2 * rows).astype(F32),
        (end_last > begin_block + 3 * rows).astype(F32),
    ]
    lane_place = lax.broadcasted_iota(jnp.int32, (rows, HEAD_DIM), 0).astype(F32) + begin_block
    first_rows = (lane_place < begin_next).astype(F32).astype(BF16)
    last_rows = (lane_place >= begin_last).astype(F32).astype(BF16)

    same = lax.broadcasted_iota(jnp.int32, (rows, docs), 0).astype(F32) + begin_block
    same = ((same >= starts) & (same < ends)).astype(F32).astype(BF16)
    same = mm(same, same, NT)
    row = lax.broadcasted_iota(jnp.int32, (rows, rows), 0)
    col = lax.broadcasted_iota(jnp.int32, (rows, rows), 1)
    pair[0] = jnp.where(col <= row, same, 0.0).astype(BF16)
    pair[1] = jnp.where(col >= row, same, 0.0).astype(BF16)

    def to(way, kind):
        if kind == 0:
            return (b >= 2, b < blocks - 2)[1 - way]
        return inside[(hops[kind], -hops[kind])[way]]

    def came(way, kind):
        if kind == 0:
            return (b >= 1) & (b < blocks - 1)
        return inside[(-hops[kind], hops[kind])[way]]

    for way in range(2):
        for kind in range(3):
            @pl.when(jnp.logical_not(came(way, kind)))
            def _():
                first[way, 2 + kind] = jnp.zeros(first.shape[2:], BF16)

    def state_copy(i, way, kind):
        return pltpu.make_async_remote_copy(
            src_ref=first.at[way, min(kind, 1), i],
            dst_ref=first.at[way, 2 + kind, i],
            send_sem=state_send.at[way, kind],
            recv_sem=state_recv.at[way, min(kind, 1), i],
            device_id={"seq": b + (hops[kind], -hops[kind])[way]},
            device_id_type=MESH,
        )

    def sent(way, kind):
        return pltpu.make_async_copy(first.at[way, 2 + kind], first.at[way, 2 + kind], state_send.at[way, kind])

    def out_copy(i, part, k):
        return pltpu.make_async_remote_copy(
            src_ref=made.at[i, parts[part], pl.ds(pl.multiple_of(peers[k] * rows_out, rows_out), rows_out), :],
            dst_ref=out_ref.at[parts[part], :, pl.ds(pl.multiple_of(h * width + i * HEAD_DIM, HEAD_DIM), HEAD_DIM)],
            send_sem=out_send,
            recv_sem=out_recv,
            device_id={"head": peers[k]},
            device_id_type=MESH,
        )

    def own_copy(i, part):
        return pltpu.make_async_copy(
            made.at[i, parts[part], pl.ds(pl.multiple_of(h * rows_out, rows_out), rows_out), :],
            out_ref.at[parts[part], :, pl.ds(pl.multiple_of(h * width + i * HEAD_DIM, HEAD_DIM), HEAD_DIM)],
            own_sem,
        )

    parts = (pl.ds(0, 1), pl.ds(1, 2))

    def states(i):
        tail = mm(v_ref[:, cols(i)], k_ref[:, cols(i)] * last_rows, TN)
        own[0, i] = tail
        first[0, 0, i] = tail.astype(BF16)
        head = mm(q_ref[:, cols(i)], g_ref[:, cols(i)] * first_rows, TN)
        own[1, i] = head
        first[1, 0, i] = head.astype(BF16)

    def send_own(i):
        for way in range(2):
            @pl.when(to(way, 0))
            def _():
                state_copy(i, way, 0).start()

    def pass_on(i):
        if i == 0:
            wait_late(after_late)
        for way in (1, 0):
            @pl.when(came(way, 0))
            def _():
                state_copy(i, way, 0).wait_recv()
            both = own[way, i] + through * first[way, 2, i].astype(F32)
            first[way, 1, i] = both.astype(BF16)
            for kind in (1, 2):
                @pl.when(to(way, kind))
                def _():
                    state_copy(i, way, kind).start()

    def inner(i):
        q, k, v, g = (ref[:, cols(i)] for ref in (q_ref, k_ref, v_ref, g_ref))
        weight = mm(g, v, NT).astype(BF16) * pair[0]
        local[0, i] = mm(weight, k, NN)
        weight = mm(v, g, NT).astype(BF16) * pair[1]
        local[1, i] = mm(weight, q, NN)
        weight = mm(k, q, NT).astype(BF16) * pair[1]
        local[2, i] = mm(weight, g, NN)

    def arrive(i, way):
        pair_in = first.at[way, pl.ds(3, 2), i]

        @pl.when(came(way, 2))
        def _():
            pltpu.make_async_copy(pair_in, pair_in, state_recv.at[way, 1, i]).wait()

        @pl.when(came(way, 1) & jnp.logical_not(came(way, 2)))
        def _():
            state_copy(i, way, 1).wait_recv()

    def whole(way, i):
        total = first[way, 3, i].astype(F32) + reach[way] * first[way, 4, i].astype(F32)
        high = total.astype(BF16)
        return high, (total - high.astype(F32)).astype(BF16)

    def send_out(i, part):
        for k in order:
            out_copy(i, part, k).start()
        own_copy(i, part).start()

    def twice(x):
        return jnp.concatenate([x, x], axis=1)

    def keys_values(i):
        high, low = whole(1, i)
        v = v_ref[:, cols(i)] * last_rows
        made[i, 1] = (local[1, i] + (mm(v, high, NT) + mm(v, low, NT))).astype(BF16)
        k = k_ref[:, cols(i)] * last_rows
        both = jnp.concatenate([high, low], axis=0)
        made[i, 2] = (local[2, i] + mm(twice(k), both, NN)).astype(BF16)

    def query(i):
        high, low = whole(0, i)
        g = g_ref[:, cols(i)] * first_rows
        both = jnp.concatenate([high, low], axis=0)
        made[i, 0] = (local[0, i] + mm(twice(g), both, NN)).astype(BF16)

    def finish(i):
        if i == 0:
            wait_late(beside_late)
        arrive(i, 1)
        keys_values(i)
        send_out(i, 1)
        arrive(i, 0)
        query(i)
        send_out(i, 0)

    loaded(0)
    states(0)
    enter()
    send_own(0)
    for i in range(1, heads):
        loaded(i)
        states(i)
        send_own(i)
    half = max(heads // 2, 1)
    for i in range(half):
        inner(i)
    for i in range(heads):
        pass_on(i)
    for i in range(half, heads):
        inner(i)
    for i in range(heads):
        finish(i)
    mine = out_ref.at[:, :, pl.ds(0, width)]
    others = out_ref.at[:, :, pl.ds(0, width * (groups - 1))]
    pltpu.make_async_copy(mine, mine, own_sem).wait()
    for way in range(2):
        for kind in range(3):
            @pl.when(to(way, kind))
            def _():
                sent(way, kind).wait()
    pltpu.make_async_copy(others, others, out_recv).wait()
    pltpu.make_async_copy(others, others, out_send).wait()


def split(whole_ref, a_ref, b_ref, c_ref, sem):
    copies = [
        pltpu.make_async_copy(whole_ref.at[i], part, sem.at[i])
        for i, part in enumerate((a_ref, b_ref, c_ref))
    ]
    for copy in copies:
        copy.start()
    for copy in copies:
        copy.wait()


def make_shards(blocks, groups):
    def shards(queries, keys, values, out_grad, doc_lengths):
        rows, width = queries.shape
        heads = width // HEAD_DIM
        rows_out = rows // groups
        docs = doc_lengths.shape[0]
        out = pl.pallas_call(
            functools.partial(kernel, blocks, groups),
            out_shape=pltpu.VMEM((3, rows_out, width * groups), BF16),
            in_specs=[pl.BlockSpec(memory_space=pltpu.HBM)] * 5,
            out_specs=pl.BlockSpec(memory_space=pltpu.VMEM),
            scratch_shapes=[pltpu.VMEM((rows, width), BF16)] * 4
            + [
                pltpu.VMEM((3, heads, rows, HEAD_DIM), F32),
                pltpu.VMEM((2, heads, HEAD_DIM, HEAD_DIM), F32),
                pltpu.VMEM((2, 5, heads, HEAD_DIM, HEAD_DIM), BF16),
                pltpu.VMEM((2, rows, rows), BF16),
                pltpu.VMEM((heads, 3, rows, HEAD_DIM), BF16),
                pltpu.VMEM((1, docs), jnp.int32),
                pltpu.SemaphoreType.DMA,
                pltpu.SemaphoreType.DMA((heads,)),
                pltpu.SemaphoreType.DMA((2, 3)),
                pltpu.SemaphoreType.DMA((2, 2, heads)),
                pltpu.SemaphoreType.DMA,
                pltpu.SemaphoreType.DMA,
                pltpu.SemaphoreType.DMA,
                pltpu.SemaphoreType.REGULAR,
            ],
            compiler_params=pltpu.CompilerParams(
                collective_id=0, has_side_effects=True
            ),
        )(queries, keys, values, out_grad, doc_lengths.reshape(1, -1))
        part = jax.ShapeDtypeStruct((rows_out, width * groups), BF16)
        return pl.pallas_call(
            split,
            out_shape=(part, part, part),
            in_specs=[pl.BlockSpec(memory_space=pltpu.VMEM)],
            out_specs=(pl.BlockSpec(memory_space=pl.ANY),) * 3,
            scratch_shapes=[pltpu.SemaphoreType.DMA((3,))],
            compiler_params=pltpu.CompilerParams(vmem_limit_bytes=8 << 20),
        )(out)

    return shards


def solution(mesh):
    return jax.shard_map(
        make_shards(mesh.shape["seq"], mesh.shape["head"]),
        mesh=mesh,
        in_specs=(P("seq", "head"), P("seq", "head"), P("seq", "head"), P("seq", "head"), P()),
        out_specs=(P(("seq", "head"), None), P(("seq", "head"), None), P(("seq", "head"), None)),
        check_vma=False,
    )
```

```python
import functools

import jax
import jax.numpy as jnp
from jax import lax
from jax.experimental import pallas as pl
from jax.experimental.pallas import tpu as pltpu
from jax.sharding import PartitionSpec as P

HEAD_DIM = 128
MESH = pl.DeviceIdType.MESH
F32 = jnp.float32
BF16 = jnp.bfloat16


NN = (((1,), (0,)), ((), ()))
NT = (((1,), (1,)), ((), ()))
TN = (((0,), (0,)), ((), ()))


def mm(a, b, dims):
    return lax.dot_general(a, b, dims, preferred_element_type=F32)


def kernel(
    blocks, groups,
    q_hbm, k_hbm, v_hbm, g_hbm, len_hbm,
    out_ref,
    q_ref, k_ref, v_ref, g_ref, local, own, first, pair, made,
    len_ref, table_sem, in_sem, state_send, state_recv, out_send, out_recv, own_sem, late_sem,
):
    rows, width = q_ref.shape
    heads = width // HEAD_DIM
    rows_out = rows // groups
    b = lax.axis_index("seq")
    h = lax.axis_index("head")

    def cols(i):
        return pl.ds(i * HEAD_DIM, HEAD_DIM)

    table_load = pltpu.make_async_copy(len_hbm, len_ref, table_sem)
    loads = [
        [
            pltpu.make_async_copy(src.at[:, cols(i)], dst.at[:, cols(i)], in_sem.at[i])
            for src, dst in ((k_hbm, k_ref), (v_hbm, v_ref), (q_hbm, q_ref), (g_hbm, g_ref))
        ]
        for i in range(heads)
    ]

    def loaded(i):
        all_four = q_ref.at[:, pl.ds(0, 4 * HEAD_DIM)]
        pltpu.make_async_copy(all_four, all_four, in_sem.at[i]).wait()

    table_load.start()
    for load in loads[0]:
        load.start()

    late = (b == 0) & (h == 0)
    shifts = (1, 3, -1, -3)
    hops = (1, 1, 3)
    inside = {s: b + s < blocks if s > 0 else b + s >= 0 for s in shifts}
    order = sorted(range(1, groups), key=lambda k: -min(k // 2, (groups - k) // 2))
    peers = {k: lax.rem(h + k, groups) for k in order}

    barrier = pltpu.get_barrier_semaphore()

    @pl.when(jnp.logical_not(late))
    def _():
        for k in order:
            pl.semaphore_signal(barrier, inc=1, device_id={"head": peers[k]}, device_id_type=MESH)
        for s in shifts:
            @pl.when(inside[s])
            def _():
                pl.semaphore_signal(barrier, inc=1, device_id={"seq": b + s}, device_id_type=MESH)

    def late_seq(s):
        return (b + s == 0) & (h == 0)

    after_late = (h == 0) & (functools.reduce(jnp.logical_or, [b == s for s in shifts if s > 0]))
    beside_late = (b == 0) & (h != 0)

    def wait_late(there):
        @pl.when(there)
        def _():
            pl.semaphore_wait(late_sem, 1)

    def enter():
        waits = len(order) + sum(inside[s].astype(jnp.int32) for s in shifts)
        waits = waits - (after_late | beside_late).astype(jnp.int32)
        pl.semaphore_wait(barrier, waits)

        @pl.when(late)
        def _():
            for k in order:
                pl.semaphore_signal(late_sem, inc=1, device_id={"head": peers[k]}, device_id_type=MESH)
            for s in shifts:
                if s > 0:
                    pl.semaphore_signal(late_sem, inc=1, device_id={"seq": b + s}, device_id_type=MESH)

    table_load.wait()

    docs = len_ref.shape[1]
    begin_block = (b * rows).astype(F32)
    lengths = jnp.broadcast_to(len_ref[...].astype(F32), (docs, docs))
    down = lax.broadcasted_iota(jnp.int32, (docs, docs), 0)
    across = lax.broadcasted_iota(jnp.int32, (docs, docs), 1)
    length_col = jnp.sum(jnp.where(down == across, lengths, 0.0), axis=1, keepdims=True)
    ends = jnp.sum(jnp.where(down <= across, length_col, 0.0), axis=0, keepdims=True)
    starts = ends - lengths[:1]
    far = 1e9
    last_place = begin_block + (rows - 1)
    begin_first = jnp.max(jnp.where(starts <= begin_block, starts, 0.0), axis=1, keepdims=True)
    begin_last = jnp.max(jnp.where(starts <= last_place, starts, 0.0), axis=1, keepdims=True)
    begin_next = jnp.min(jnp.where(starts >= begin_block, starts, far), axis=1, keepdims=True)
    end_last = jnp.min(jnp.where(ends > last_place, ends, far), axis=1, keepdims=True)
    through = (begin_last < begin_block).astype(F32)
    reach = [
        (begin_first < begin_block - 2 * rows).astype(F32),
        (end_last > begin_block + 3 * rows).astype(F32),
    ]
    lane_place = lax.broadcasted_iota(jnp.int32, (rows, HEAD_DIM), 0).astype(F32) + begin_block
    first_rows = (lane_place < begin_next).astype(F32).astype(BF16)
    last_rows = (lane_place >= begin_last).astype(F32).astype(BF16)

    def to(way, kind):
        if kind == 0:
            return (b >= 2, b < blocks - 2)[1 - way]
        return inside[(hops[kind], -hops[kind])[way]]

    def came(way, kind):
        if kind == 0:
            return (b >= 1) & (b < blocks - 1)
        return inside[(-hops[kind], hops[kind])[way]]

    for way in range(2):
        for kind in range(3):
            @pl.when(jnp.logical_not(came(way, kind)))
            def _():
                first[way, 2 + kind] = jnp.zeros(first.shape[2:], BF16)

    def state_copy(i, way, kind):
        return pltpu.make_async_remote_copy(
            src_ref=first.at[way, min(kind, 1), i],
            dst_ref=first.at[way, 2 + kind, i],
            send_sem=state_send.at[way, kind],
            recv_sem=state_recv.at[way, min(kind, 1), i],
            device_id={"seq": b + (hops[kind], -hops[kind])[way]},
            device_id_type=MESH,
        )

    def sent(way, kind):
        return pltpu.make_async_copy(first.at[way, 2 + kind], first.at[way, 2 + kind], state_send.at[way, kind])

    def out_copy(i, part, k):
        return pltpu.make_async_remote_copy(
            src_ref=made.at[i, parts[part], pl.ds(pl.multiple_of(peers[k] * rows_out, rows_out), rows_out), :],
            dst_ref=out_ref.at[parts[part], :, pl.ds(pl.multiple_of(h * width + i * HEAD_DIM, HEAD_DIM), HEAD_DIM)],
            send_sem=out_send,
            recv_sem=out_recv,
            device_id={"head": peers[k]},
            device_id_type=MESH,
        )

    def own_copy(i, part):
        return pltpu.make_async_copy(
            made.at[i, parts[part], pl.ds(pl.multiple_of(h * rows_out, rows_out), rows_out), :],
            out_ref.at[parts[part], :, pl.ds(pl.multiple_of(h * width + i * HEAD_DIM, HEAD_DIM), HEAD_DIM)],
            own_sem,
        )

    parts = (pl.ds(0, 1), pl.ds(1, 2))

    def states(i):
        tail = mm(v_ref[:, cols(i)], k_ref[:, cols(i)] * last_rows, TN)
        own[0, i] = tail
        first[0, 0, i] = tail.astype(BF16)
        head = mm(q_ref[:, cols(i)], g_ref[:, cols(i)] * first_rows, TN)
        own[1, i] = head
        first[1, 0, i] = head.astype(BF16)

    def send_own(i):
        for way in range(2):
            @pl.when(to(way, 0))
            def _():
                state_copy(i, way, 0).start()

    def pass_on(i):
        if i == 0:
            wait_late(after_late)
        for way in (0, 1):
            @pl.when(came(way, 0))
            def _():
                state_copy(i, way, 0).wait_recv()
            both = own[way, i] + through * first[way, 2, i].astype(F32)
            first[way, 1, i] = both.astype(BF16)
            for kind in (1, 2):
                @pl.when(to(way, kind))
                def _():
                    state_copy(i, way, kind).start()

    def inner(i):
        q, k, v, g = (ref[:, cols(i)] for ref in (q_ref, k_ref, v_ref, g_ref))
        weight = mm(g, v, NT).astype(BF16) * pair[0]
        local[0, i] = mm(weight, k, NN)
        weight = mm(v, g, NT).astype(BF16) * pair[1]
        local[1, i] = mm(weight, q, NN)
        weight = mm(k, q, NT).astype(BF16) * pair[1]
        local[2, i] = mm(weight, g, NN)

    def arrive(i, way):
        pair_in = first.at[way, pl.ds(3, 2), i]

        @pl.when(came(way, 2))
        def _():
            pltpu.make_async_copy(pair_in, pair_in, state_recv.at[way, 1, i]).wait()

        @pl.when(came(way, 1) & jnp.logical_not(came(way, 2)))
        def _():
            state_copy(i, way, 1).wait_recv()

    def whole(way, i):
        total = first[way, 3, i].astype(F32) + reach[way] * first[way, 4, i].astype(F32)
        high = total.astype(BF16)
        return high, (total - high.astype(F32)).astype(BF16)

    def send_out(i, part):
        for k in order:
            out_copy(i, part, k).start()
        own_copy(i, part).start()

    def twice(x):
        return jnp.concatenate([x, x], axis=1)

    def keys_values(i):
        high, low = whole(1, i)
        v = v_ref[:, cols(i)] * last_rows
        made[i, 1] = (local[1, i] + (mm(v, high, NT) + mm(v, low, NT))).astype(BF16)
        k = k_ref[:, cols(i)] * last_rows
        both = jnp.concatenate([high, low], axis=0)
        made[i, 2] = (local[2, i] + mm(twice(k), both, NN)).astype(BF16)

    def query(i):
        high, low = whole(0, i)
        g = g_ref[:, cols(i)] * first_rows
        both = jnp.concatenate([high, low], axis=0)
        made[i, 0] = (local[0, i] + mm(twice(g), both, NN)).astype(BF16)

    def finish(i):
        if i == 0:
            wait_late(beside_late)
        arrive(i, 0)
        query(i)
        send_out(i, 0)
        arrive(i, 1)
        keys_values(i)
        send_out(i, 1)

    loaded(0)
    for load in sum(loads[1:], []):
        load.start()
    states(0)
    enter()
    send_own(0)
    for i in range(1, heads):
        loaded(i)
        states(i)
        send_own(i)
    same = lax.broadcasted_iota(jnp.int32, (rows, docs), 0).astype(F32) + begin_block
    same = ((same >= starts) & (same < ends)).astype(F32).astype(BF16)
    same = mm(same, same, NT)
    row = lax.broadcasted_iota(jnp.int32, (rows, rows), 0)
    col = lax.broadcasted_iota(jnp.int32, (rows, rows), 1)
    pair[0] = jnp.where(col <= row, same, 0.0).astype(BF16)
    pair[1] = jnp.where(col >= row, same, 0.0).astype(BF16)

    half = 1
    for i in range(half):
        inner(i)
    for i in range(heads):
        pass_on(i)
    for i in range(half, heads):
        inner(i)
    for i in range(heads):
        finish(i)
    mine = out_ref.at[:, :, pl.ds(0, width)]
    others = out_ref.at[:, :, pl.ds(0, width * (groups - 1))]
    pltpu.make_async_copy(mine, mine, own_sem).wait()
    for way in range(2):
        for kind in range(3):
            @pl.when(to(way, kind))
            def _():
                sent(way, kind).wait()
    pltpu.make_async_copy(others, others, out_recv).wait()
    pltpu.make_async_copy(others, others, out_send).wait()


def split(whole_ref, a_ref, b_ref, c_ref, sem):
    half = a_ref.shape[0] // 2
    for i, part in enumerate((a_ref, b_ref, c_ref)):
        for j in range(2):
            some = pl.ds(j * half, half)
            pltpu.make_async_copy(whole_ref.at[i, some], part.at[some], sem).start()
    pltpu.make_async_copy(whole_ref, whole_ref, sem).wait()


def make_shards(blocks, groups):
    def shards(queries, keys, values, out_grad, doc_lengths):
        rows, width = queries.shape
        heads = width // HEAD_DIM
        rows_out = rows // groups
        docs = doc_lengths.shape[0]
        out = pl.pallas_call(
            functools.partial(kernel, blocks, groups),
            out_shape=pltpu.VMEM((3, rows_out, width * groups), BF16),
            in_specs=[pl.BlockSpec(memory_space=pltpu.HBM)] * 5,
            out_specs=pl.BlockSpec(memory_space=pltpu.VMEM),
            scratch_shapes=[pltpu.VMEM((rows, width), BF16)] * 4
            + [
                pltpu.VMEM((3, heads, rows, HEAD_DIM), F32),
                pltpu.VMEM((2, heads, HEAD_DIM, HEAD_DIM), F32),
                pltpu.VMEM((2, 5, heads, HEAD_DIM, HEAD_DIM), BF16),
                pltpu.VMEM((2, rows, rows), BF16),
                pltpu.VMEM((heads, 3, rows, HEAD_DIM), BF16),
                pltpu.VMEM((1, docs), jnp.int32),
                pltpu.SemaphoreType.DMA,
                pltpu.SemaphoreType.DMA((heads,)),
                pltpu.SemaphoreType.DMA((2, 3)),
                pltpu.SemaphoreType.DMA((2, 2, heads)),
                pltpu.SemaphoreType.DMA,
                pltpu.SemaphoreType.DMA,
                pltpu.SemaphoreType.DMA,
                pltpu.SemaphoreType.REGULAR,
            ],
            compiler_params=pltpu.CompilerParams(
                collective_id=0, has_side_effects=True
            ),
        )(queries, keys, values, out_grad, doc_lengths.reshape(1, -1))
        part = jax.ShapeDtypeStruct((rows_out, width * groups), BF16)
        return pl.pallas_call(
            split,
            out_shape=(part, part, part),
            in_specs=[pl.BlockSpec(memory_space=pltpu.VMEM)],
            out_specs=(pl.BlockSpec(memory_space=pl.ANY),) * 3,
            scratch_shapes=[pltpu.SemaphoreType.DMA],
            compiler_params=pltpu.CompilerParams(vmem_limit_bytes=8 << 20),
        )(out)

    return shards


def solution(mesh):
    return jax.shard_map(
        make_shards(mesh.shape["seq"], mesh.shape["head"]),
        mesh=mesh,
        in_specs=(P("seq", "head"), P("seq", "head"), P("seq", "head"), P("seq", "head"), P()),
        out_specs=(P(("seq", "head"), None), P(("seq", "head"), None), P(("seq", "head"), None)),
        check_vma=False,
    )
```

```python
import functools

import jax
import jax.numpy as jnp
from jax import lax
from jax.experimental import pallas as pl
from jax.experimental.pallas import tpu as pltpu
from jax.sharding import PartitionSpec as P

HEAD_DIM = 128
MESH = pl.DeviceIdType.MESH
F32 = jnp.float32
BF16 = jnp.bfloat16


NN = (((1,), (0,)), ((), ()))
NT = (((1,), (1,)), ((), ()))
TN = (((0,), (0,)), ((), ()))


def mm(a, b, dims):
    return lax.dot_general(a, b, dims, preferred_element_type=F32)


def kernel(
    blocks, groups,
    q_hbm, k_hbm, v_hbm, g_hbm, len_hbm,
    out_ref,
    q_ref, k_ref, v_ref, g_ref, local, own, first, pair, made,
    len_ref, table_sem, in_sem, state_send, state_recv, out_send, out_recv, own_sem, late_sem,
):
    rows, width = q_ref.shape
    heads = width // HEAD_DIM
    rows_out = rows // groups
    b = lax.axis_index("seq")
    h = lax.axis_index("head")

    def cols(i):
        return pl.ds(i * HEAD_DIM, HEAD_DIM)

    table_load = pltpu.make_async_copy(len_hbm, len_ref, table_sem)
    loads = [
        [
            pltpu.make_async_copy(src.at[:, cols(i)], dst.at[:, cols(i)], in_sem.at[i])
            for src, dst in ((k_hbm, k_ref), (v_hbm, v_ref), (q_hbm, q_ref), (g_hbm, g_ref))
        ]
        for i in range(heads)
    ]

    def loaded(i):
        all_four = q_ref.at[:, pl.ds(0, 4 * HEAD_DIM)]
        pltpu.make_async_copy(all_four, all_four, in_sem.at[i]).wait()

    table_load.start()
    for load in loads[0]:
        load.start()

    late = (b == 0) & (h == 0)
    shifts = (1, 3, -1, -3)
    hops = (1, 1, 3)
    inside = {s: b + s < blocks if s > 0 else b + s >= 0 for s in shifts}
    order = sorted(range(1, groups), key=lambda k: -min(k // 2, (groups - k) // 2))
    peers = {k: lax.rem(h + k, groups) for k in order}

    barrier = pltpu.get_barrier_semaphore()

    @pl.when(jnp.logical_not(late))
    def _():
        for k in order:
            pl.semaphore_signal(barrier, inc=1, device_id={"head": peers[k]}, device_id_type=MESH)
        for s in shifts:
            @pl.when(inside[s])
            def _():
                pl.semaphore_signal(barrier, inc=1, device_id={"seq": b + s}, device_id_type=MESH)

    def late_seq(s):
        return (b + s == 0) & (h == 0)

    after_late = (h == 0) & (functools.reduce(jnp.logical_or, [b == s for s in shifts if s > 0]))
    beside_late = (b == 0) & (h != 0)

    def wait_late(there):
        @pl.when(there)
        def _():
            pl.semaphore_wait(late_sem, 1)

    def enter():
        waits = len(order) + sum(inside[s].astype(jnp.int32) for s in shifts)
        waits = waits - (after_late | beside_late).astype(jnp.int32)
        pl.semaphore_wait(barrier, waits)

        @pl.when(late)
        def _():
            for k in order:
                pl.semaphore_signal(late_sem, inc=1, device_id={"head": peers[k]}, device_id_type=MESH)
            for s in shifts:
                if s > 0:
                    pl.semaphore_signal(late_sem, inc=1, device_id={"seq": b + s}, device_id_type=MESH)

    table_load.wait()

    docs = len_ref.shape[1]
    begin_block = (b * rows).astype(F32)
    lengths = jnp.broadcast_to(len_ref[...].astype(F32), (docs, docs))
    down = lax.broadcasted_iota(jnp.int32, (docs, docs), 0)
    across = lax.broadcasted_iota(jnp.int32, (docs, docs), 1)
    length_col = jnp.sum(jnp.where(down == across, lengths, 0.0), axis=1, keepdims=True)
    ends = jnp.sum(jnp.where(down <= across, length_col, 0.0), axis=0, keepdims=True)
    starts = ends - lengths[:1]
    far = 1e9
    last_place = begin_block + (rows - 1)
    begin_first = jnp.max(jnp.where(starts <= begin_block, starts, 0.0), axis=1, keepdims=True)
    begin_last = jnp.max(jnp.where(starts <= last_place, starts, 0.0), axis=1, keepdims=True)
    begin_next = jnp.min(jnp.where(starts >= begin_block, starts, far), axis=1, keepdims=True)
    end_last = jnp.min(jnp.where(ends > last_place, ends, far), axis=1, keepdims=True)
    through = (begin_last < begin_block).astype(F32)
    reach = [
        (begin_first < begin_block - 2 * rows).astype(F32),
        (end_last > begin_block + 3 * rows).astype(F32),
    ]
    lane_place = lax.broadcasted_iota(jnp.int32, (rows, HEAD_DIM), 0).astype(F32) + begin_block
    first_rows = (lane_place < begin_next).astype(F32).astype(BF16)
    last_rows = (lane_place >= begin_last).astype(F32).astype(BF16)

    def to(way, kind):
        if kind == 0:
            return (b >= 2, b < blocks - 2)[1 - way]
        return inside[(hops[kind], -hops[kind])[way]]

    def came(way, kind):
        if kind == 0:
            return (b >= 1) & (b < blocks - 1)
        return inside[(-hops[kind], hops[kind])[way]]

    for way in range(2):
        for kind in range(3):
            @pl.when(jnp.logical_not(came(way, kind)))
            def _():
                first[way, 2 + kind] = jnp.zeros(first.shape[2:], BF16)

    def state_copy(i, way, kind):
        return pltpu.make_async_remote_copy(
            src_ref=first.at[way, min(kind, 1), i],
            dst_ref=first.at[way, 2 + kind, i],
            send_sem=state_send.at[way, kind],
            recv_sem=state_recv.at[way, min(kind, 1), i],
            device_id={"seq": b + (hops[kind], -hops[kind])[way]},
            device_id_type=MESH,
        )

    def sent(way, kind):
        return pltpu.make_async_copy(first.at[way, 2 + kind], first.at[way, 2 + kind], state_send.at[way, kind])

    def out_copy(i, part, k):
        return pltpu.make_async_remote_copy(
            src_ref=made.at[i, parts[part], pl.ds(pl.multiple_of(peers[k] * rows_out, rows_out), rows_out), :],
            dst_ref=out_ref.at[parts[part], :, pl.ds(pl.multiple_of(h * width + i * HEAD_DIM, HEAD_DIM), HEAD_DIM)],
            send_sem=out_send,
            recv_sem=out_recv,
            device_id={"head": peers[k]},
            device_id_type=MESH,
        )

    def own_copy(i, part):
        return pltpu.make_async_copy(
            made.at[i, parts[part], pl.ds(pl.multiple_of(h * rows_out, rows_out), rows_out), :],
            out_ref.at[parts[part], :, pl.ds(pl.multiple_of(h * width + i * HEAD_DIM, HEAD_DIM), HEAD_DIM)],
            own_sem,
        )

    parts = (pl.ds(0, 1), pl.ds(1, 2))

    def states(i):
        tail = mm(v_ref[:, cols(i)], k_ref[:, cols(i)] * last_rows, TN)
        own[0, i] = tail
        first[0, 0, i] = tail.astype(BF16)
        head = mm(q_ref[:, cols(i)], g_ref[:, cols(i)] * first_rows, TN)
        own[1, i] = head
        first[1, 0, i] = head.astype(BF16)

    def send_own(i):
        for way in range(2):
            @pl.when(to(way, 0))
            def _():
                state_copy(i, way, 0).start()

    def pass_on(i):
        if i == 0:
            wait_late(after_late)
        for way in (0, 1):
            @pl.when(came(way, 0))
            def _():
                state_copy(i, way, 0).wait_recv()
            both = own[way, i] + through * first[way, 2, i].astype(F32)
            first[way, 1, i] = both.astype(BF16)
            for kind in (1, 2):
                @pl.when(to(way, kind))
                def _():
                    state_copy(i, way, kind).start()

    def inner(i):
        q, k, v, g = (ref[:, cols(i)] for ref in (q_ref, k_ref, v_ref, g_ref))
        weight = mm(g, v, NT).astype(BF16) * pair[0]
        local[0, i] = mm(weight, k, NN)
        weight = mm(v, g, NT).astype(BF16) * pair[1]
        local[1, i] = mm(weight, q, NN)
        weight = mm(k, q, NT).astype(BF16) * pair[1]
        local[2, i] = mm(weight, g, NN)

    def arrive(i, way):
        pair_in = first.at[way, pl.ds(3, 2), i]

        @pl.when(came(way, 2))
        def _():
            pltpu.make_async_copy(pair_in, pair_in, state_recv.at[way, 1, i]).wait()

        @pl.when(came(way, 1) & jnp.logical_not(came(way, 2)))
        def _():
            state_copy(i, way, 1).wait_recv()

    def whole(way, i):
        total = first[way, 3, i].astype(F32) + reach[way] * first[way, 4, i].astype(F32)
        high = total.astype(BF16)
        return high, (total - high.astype(F32)).astype(BF16)

    def send_out(i, part):
        for k in order:
            out_copy(i, part, k).start()
        own_copy(i, part).start()

    def twice(x):
        return jnp.concatenate([x, x], axis=1)

    def keys_values(i):
        high, low = whole(1, i)
        v = v_ref[:, cols(i)] * last_rows
        made[i, 1] = (local[1, i] + (mm(v, high, NT) + mm(v, low, NT))).astype(BF16)
        k = k_ref[:, cols(i)] * last_rows
        both = jnp.concatenate([high, low], axis=0)
        made[i, 2] = (local[2, i] + mm(twice(k), both, NN)).astype(BF16)

    def query(i):
        high, low = whole(0, i)
        g = g_ref[:, cols(i)] * first_rows
        both = jnp.concatenate([high, low], axis=0)
        made[i, 0] = (local[0, i] + mm(twice(g), both, NN)).astype(BF16)

    def finish(i):
        if i == 0:
            wait_late(beside_late)
        for part in (1, 0) if i == heads - 1 else (0, 1):
            arrive(i, part)
            (query, keys_values)[part](i)
            send_out(i, part)

    loaded(0)
    for load in sum(loads[1:], []):
        load.start()
    states(0)
    enter()
    send_own(0)
    for i in range(1, heads):
        loaded(i)
        states(i)
        send_own(i)
    same = lax.broadcasted_iota(jnp.int32, (rows, docs), 0).astype(F32) + begin_block
    same = ((same >= starts) & (same < ends)).astype(F32).astype(BF16)
    same = mm(same, same, NT)
    row = lax.broadcasted_iota(jnp.int32, (rows, rows), 0)
    col = lax.broadcasted_iota(jnp.int32, (rows, rows), 1)
    pair[0] = jnp.where(col <= row, same, 0.0).astype(BF16)
    pair[1] = jnp.where(col >= row, same, 0.0).astype(BF16)

    half = 1
    for i in range(half):
        inner(i)
    for i in range(heads):
        pass_on(i)
    for i in range(half, heads):
        inner(i)
    for i in range(heads):
        finish(i)
    mine = out_ref.at[:, :, pl.ds(0, width)]
    others = out_ref.at[:, :, pl.ds(0, width * (groups - 1))]
    pltpu.make_async_copy(mine, mine, own_sem).wait()
    for way in range(2):
        for kind in range(3):
            @pl.when(to(way, kind))
            def _():
                sent(way, kind).wait()
    pltpu.make_async_copy(others, others, out_recv).wait()
    pltpu.make_async_copy(others, others, out_send).wait()


def split(whole_ref, a_ref, b_ref, c_ref, sem):
    half = a_ref.shape[0] // 2
    for i, part in enumerate((a_ref, b_ref, c_ref)):
        for j in range(2):
            some = pl.ds(j * half, half)
            pltpu.make_async_copy(whole_ref.at[i, some], part.at[some], sem).start()
    pltpu.make_async_copy(whole_ref, whole_ref, sem).wait()


def make_shards(blocks, groups):
    def shards(queries, keys, values, out_grad, doc_lengths):
        rows, width = queries.shape
        heads = width // HEAD_DIM
        rows_out = rows // groups
        docs = doc_lengths.shape[0]
        out = pl.pallas_call(
            functools.partial(kernel, blocks, groups),
            out_shape=pltpu.VMEM((3, rows_out, width * groups), BF16),
            in_specs=[pl.BlockSpec(memory_space=pltpu.HBM)] * 5,
            out_specs=pl.BlockSpec(memory_space=pltpu.VMEM),
            scratch_shapes=[pltpu.VMEM((rows, width), BF16)] * 4
            + [
                pltpu.VMEM((3, heads, rows, HEAD_DIM), F32),
                pltpu.VMEM((2, heads, HEAD_DIM, HEAD_DIM), F32),
                pltpu.VMEM((2, 5, heads, HEAD_DIM, HEAD_DIM), BF16),
                pltpu.VMEM((2, rows, rows), BF16),
                pltpu.VMEM((heads, 3, rows, HEAD_DIM), BF16),
                pltpu.VMEM((1, docs), jnp.int32),
                pltpu.SemaphoreType.DMA,
                pltpu.SemaphoreType.DMA((heads,)),
                pltpu.SemaphoreType.DMA((2, 3)),
                pltpu.SemaphoreType.DMA((2, 2, heads)),
                pltpu.SemaphoreType.DMA,
                pltpu.SemaphoreType.DMA,
                pltpu.SemaphoreType.DMA,
                pltpu.SemaphoreType.REGULAR,
            ],
            compiler_params=pltpu.CompilerParams(
                collective_id=0, has_side_effects=True
            ),
        )(queries, keys, values, out_grad, doc_lengths.reshape(1, -1))
        part = jax.ShapeDtypeStruct((rows_out, width * groups), BF16)
        return pl.pallas_call(
            split,
            out_shape=(part, part, part),
            in_specs=[pl.BlockSpec(memory_space=pltpu.VMEM)],
            out_specs=(pl.BlockSpec(memory_space=pl.ANY),) * 3,
            scratch_shapes=[pltpu.SemaphoreType.DMA],
            compiler_params=pltpu.CompilerParams(vmem_limit_bytes=8 << 20),
        )(out)

    return shards


def solution(mesh):
    return jax.shard_map(
        make_shards(mesh.shape["seq"], mesh.shape["head"]),
        mesh=mesh,
        in_specs=(P("seq", "head"), P("seq", "head"), P("seq", "head"), P("seq", "head"), P()),
        out_specs=(P(("seq", "head"), None), P(("seq", "head"), None), P(("seq", "head"), None)),
        check_vma=False,
    )
```

```python
import functools

import jax
import jax.numpy as jnp
from jax import lax
from jax.experimental import pallas as pl
from jax.experimental.pallas import tpu as pltpu
from jax.sharding import PartitionSpec as P

HEAD_DIM = 128
MESH = pl.DeviceIdType.MESH
F32 = jnp.float32
BF16 = jnp.bfloat16


NN = (((1,), (0,)), ((), ()))
NT = (((1,), (1,)), ((), ()))
TN = (((0,), (0,)), ((), ()))


def mm(a, b, dims):
    return lax.dot_general(a, b, dims, preferred_element_type=F32)


def kernel(
    blocks, groups,
    q_hbm, k_hbm, v_hbm, g_hbm, len_hbm,
    out_ref,
    q_ref, k_ref, v_ref, g_ref, local, own, first, pair, made,
    len_ref, table_sem, in_sem, state_send, state_recv, out_send, out_recv, own_sem, late_sem,
):
    rows, width = q_ref.shape
    heads = width // HEAD_DIM
    rows_out = rows // groups
    b = lax.axis_index("seq")
    h = lax.axis_index("head")

    def cols(i):
        return pl.ds(i * HEAD_DIM, HEAD_DIM)

    table_load = pltpu.make_async_copy(len_hbm, len_ref, table_sem)
    loads = [
        [
            pltpu.make_async_copy(src.at[:, cols(i)], dst.at[:, cols(i)], in_sem.at[i])
            for src, dst in ((k_hbm, k_ref), (v_hbm, v_ref), (q_hbm, q_ref), (g_hbm, g_ref))
        ]
        for i in range(heads)
    ]

    def loaded(i):
        all_four = q_ref.at[:, pl.ds(0, 4 * HEAD_DIM)]
        pltpu.make_async_copy(all_four, all_four, in_sem.at[i]).wait()

    table_load.start()
    for load in loads[0]:
        load.start()

    late = (b == 0) & (h == 0)
    shifts = (1, 3, -1, -3)
    hops = (1, 1, 3)
    inside = {s: b + s < blocks if s > 0 else b + s >= 0 for s in shifts}
    order = sorted(range(1, groups), key=lambda k: -min(k // 2, (groups - k) // 2))
    peers = {k: lax.rem(h + k, groups) for k in order}

    barrier = pltpu.get_barrier_semaphore()

    @pl.when(jnp.logical_not(late))
    def _():
        for k in order:
            pl.semaphore_signal(barrier, inc=1, device_id={"head": peers[k]}, device_id_type=MESH)
        for s in shifts:
            @pl.when(inside[s])
            def _():
                pl.semaphore_signal(barrier, inc=1, device_id={"seq": b + s}, device_id_type=MESH)

    def late_seq(s):
        return (b + s == 0) & (h == 0)

    after_late = (h == 0) & (functools.reduce(jnp.logical_or, [b == s for s in shifts if s > 0]))
    beside_late = (b == 0) & (h != 0)

    def wait_late(there):
        @pl.when(there)
        def _():
            pl.semaphore_wait(late_sem, 1)

    def enter():
        waits = len(order) + sum(inside[s].astype(jnp.int32) for s in shifts)
        waits = waits - (after_late | beside_late).astype(jnp.int32)
        pl.semaphore_wait(barrier, waits)

        @pl.when(late)
        def _():
            for k in order:
                pl.semaphore_signal(late_sem, inc=1, device_id={"head": peers[k]}, device_id_type=MESH)
            for s in shifts:
                if s > 0:
                    pl.semaphore_signal(late_sem, inc=1, device_id={"seq": b + s}, device_id_type=MESH)

    table_load.wait()

    docs = len_ref.shape[1]
    begin_block = (b * rows).astype(F32)
    lengths = jnp.broadcast_to(len_ref[...].astype(F32), (docs, docs))
    down = lax.broadcasted_iota(jnp.int32, (docs, docs), 0)
    across = lax.broadcasted_iota(jnp.int32, (docs, docs), 1)
    length_col = jnp.sum(jnp.where(down == across, lengths, 0.0), axis=1, keepdims=True)
    ends = jnp.sum(jnp.where(down <= across, length_col, 0.0), axis=0, keepdims=True)
    starts = ends - lengths[:1]
    far = 1e9
    last_place = begin_block + (rows - 1)
    begin_first = jnp.max(jnp.where(starts <= begin_block, starts, 0.0), axis=1, keepdims=True)
    begin_last = jnp.max(jnp.where(starts <= last_place, starts, 0.0), axis=1, keepdims=True)
    begin_next = jnp.min(jnp.where(starts >= begin_block, starts, far), axis=1, keepdims=True)
    end_last = jnp.min(jnp.where(ends > last_place, ends, far), axis=1, keepdims=True)
    through = (begin_last < begin_block).astype(F32)
    reach = [
        (begin_first < begin_block - 2 * rows).astype(F32),
        (end_last > begin_block + 3 * rows).astype(F32),
    ]
    lane_place = lax.broadcasted_iota(jnp.int32, (rows, HEAD_DIM), 0).astype(F32) + begin_block
    first_rows = (lane_place < begin_next).astype(F32).astype(BF16)
    last_rows = (lane_place >= begin_last).astype(F32).astype(BF16)

    def to(way, kind):
        if kind == 0:
            return (b >= 2, b < blocks - 2)[1 - way]
        return inside[(hops[kind], -hops[kind])[way]]

    def came(way, kind):
        if kind == 0:
            return (b >= 1) & (b < blocks - 1)
        return inside[(-hops[kind], hops[kind])[way]]

    for way in range(2):
        for kind in range(3):
            @pl.when(jnp.logical_not(came(way, kind)))
            def _():
                first[way, 2 + kind] = jnp.zeros(first.shape[2:], BF16)

    def state_copy(i, way, kind):
        return pltpu.make_async_remote_copy(
            src_ref=first.at[way, min(kind, 1), i],
            dst_ref=first.at[way, 2 + kind, i],
            send_sem=state_send.at[way, kind],
            recv_sem=state_recv.at[way, min(kind, 1), i],
            device_id={"seq": b + (hops[kind], -hops[kind])[way]},
            device_id_type=MESH,
        )

    def sent(way, kind):
        return pltpu.make_async_copy(first.at[way, 2 + kind], first.at[way, 2 + kind], state_send.at[way, kind])

    def out_copy(i, part, k):
        return pltpu.make_async_remote_copy(
            src_ref=made.at[i, parts[part], pl.ds(pl.multiple_of(peers[k] * rows_out, rows_out), rows_out), :],
            dst_ref=out_ref.at[parts[part], :, pl.ds(pl.multiple_of(h * width + i * HEAD_DIM, HEAD_DIM), HEAD_DIM)],
            send_sem=out_send,
            recv_sem=out_recv,
            device_id={"head": peers[k]},
            device_id_type=MESH,
        )

    def own_copy(i, part):
        return pltpu.make_async_copy(
            made.at[i, parts[part], pl.ds(pl.multiple_of(h * rows_out, rows_out), rows_out), :],
            out_ref.at[parts[part], :, pl.ds(pl.multiple_of(h * width + i * HEAD_DIM, HEAD_DIM), HEAD_DIM)],
            own_sem,
        )

    parts = (pl.ds(0, 1), pl.ds(1, 2))

    def states(i):
        tail = mm(v_ref[:, cols(i)], k_ref[:, cols(i)] * last_rows, TN)
        own[0, i] = tail
        first[0, 0, i] = tail.astype(BF16)
        head = mm(q_ref[:, cols(i)], g_ref[:, cols(i)] * first_rows, TN)
        own[1, i] = head
        first[1, 0, i] = head.astype(BF16)

    def send_own(i):
        for way in range(2):
            @pl.when(to(way, 0))
            def _():
                state_copy(i, way, 0).start()

    def pass_on(i):
        if i == 0:
            wait_late(after_late)
        for way in (0, 1):
            @pl.when(came(way, 0))
            def _():
                state_copy(i, way, 0).wait_recv()
            both = own[way, i] + through * first[way, 2, i].astype(F32)
            first[way, 1, i] = both.astype(BF16)
            for kind in (1, 2):
                @pl.when(to(way, kind))
                def _():
                    state_copy(i, way, kind).start()

    def inner(i):
        q, k, v, g = (ref[:, cols(i)] for ref in (q_ref, k_ref, v_ref, g_ref))
        weight = mm(g, v, NT).astype(BF16) * pair[0]
        local[0, i] = mm(weight, k, NN)
        weight = mm(v, g, NT).astype(BF16) * pair[1]
        local[1, i] = mm(weight, q, NN)
        weight = mm(k, q, NT).astype(BF16) * pair[1]
        local[2, i] = mm(weight, g, NN)

    def arrive(i, way):
        pair_in = first.at[way, pl.ds(3, 2), i]

        @pl.when(came(way, 2))
        def _():
            pltpu.make_async_copy(pair_in, pair_in, state_recv.at[way, 1, i]).wait()

        @pl.when(came(way, 1) & jnp.logical_not(came(way, 2)))
        def _():
            state_copy(i, way, 1).wait_recv()

    def whole(way, i):
        total = first[way, 3, i].astype(F32) + reach[way] * first[way, 4, i].astype(F32)
        high = total.astype(BF16)
        return high, (total - high.astype(F32)).astype(BF16)

    def send_out(i, part):
        for k in order:
            out_copy(i, part, k).start()
        own_copy(i, part).start()

    def twice(x):
        return jnp.concatenate([x, x], axis=1)

    def keys_values(i):
        high, low = whole(1, i)
        v = v_ref[:, cols(i)] * last_rows
        made[i, 1] = (local[1, i] + mm(twice(v), jnp.concatenate([high, low], axis=1), NT)).astype(BF16)
        k = k_ref[:, cols(i)] * last_rows
        both = jnp.concatenate([high, low], axis=0)
        made[i, 2] = (local[2, i] + mm(twice(k), both, NN)).astype(BF16)

    def query(i):
        high, low = whole(0, i)
        g = g_ref[:, cols(i)] * first_rows
        both = jnp.concatenate([high, low], axis=0)
        made[i, 0] = (local[0, i] + mm(twice(g), both, NN)).astype(BF16)

    def finish(i):
        if i == 0:
            wait_late(beside_late)
        for part in (1, 0) if i == heads - 1 else (0, 1):
            arrive(i, part)
            (query, keys_values)[part](i)
            send_out(i, part)

    loaded(0)
    for load in sum(loads[1:], []):
        load.start()
    states(0)
    enter()
    send_own(0)
    for i in range(1, heads):
        loaded(i)
        states(i)
        send_own(i)
    same = lax.broadcasted_iota(jnp.int32, (rows, docs), 0).astype(F32) + begin_block
    same = ((same >= starts) & (same < ends)).astype(F32).astype(BF16)
    same = mm(same, same, NT)
    row = lax.broadcasted_iota(jnp.int32, (rows, rows), 0)
    col = lax.broadcasted_iota(jnp.int32, (rows, rows), 1)
    pair[0] = jnp.where(col <= row, same, 0.0).astype(BF16)
    pair[1] = jnp.where(col >= row, same, 0.0).astype(BF16)

    half = 1
    for i in range(half):
        inner(i)
    for i in range(heads):
        pass_on(i)
    for i in range(half, heads):
        inner(i)
    for i in range(heads):
        finish(i)
    mine = out_ref.at[:, :, pl.ds(0, width)]
    others = out_ref.at[:, :, pl.ds(0, width * (groups - 1))]
    pltpu.make_async_copy(mine, mine, own_sem).wait()
    for way in range(2):
        for kind in range(3):
            @pl.when(to(way, kind))
            def _():
                sent(way, kind).wait()
    pltpu.make_async_copy(others, others, out_recv).wait()
    pltpu.make_async_copy(others, others, out_send).wait()


def split(whole_ref, a_ref, b_ref, c_ref, sem):
    half = a_ref.shape[0] // 2
    for i, part in enumerate((a_ref, b_ref, c_ref)):
        for j in range(2):
            some = pl.ds(j * half, half)
            pltpu.make_async_copy(whole_ref.at[i, some], part.at[some], sem).start()
    pltpu.make_async_copy(whole_ref, whole_ref, sem).wait()


def make_shards(blocks, groups):
    def shards(queries, keys, values, out_grad, doc_lengths):
        rows, width = queries.shape
        heads = width // HEAD_DIM
        rows_out = rows // groups
        docs = doc_lengths.shape[0]
        out = pl.pallas_call(
            functools.partial(kernel, blocks, groups),
            out_shape=pltpu.VMEM((3, rows_out, width * groups), BF16),
            in_specs=[pl.BlockSpec(memory_space=pltpu.HBM)] * 5,
            out_specs=pl.BlockSpec(memory_space=pltpu.VMEM),
            scratch_shapes=[pltpu.VMEM((rows, width), BF16)] * 4
            + [
                pltpu.VMEM((3, heads, rows, HEAD_DIM), F32),
                pltpu.VMEM((2, heads, HEAD_DIM, HEAD_DIM), F32),
                pltpu.VMEM((2, 5, heads, HEAD_DIM, HEAD_DIM), BF16),
                pltpu.VMEM((2, rows, rows), BF16),
                pltpu.VMEM((heads, 3, rows, HEAD_DIM), BF16),
                pltpu.VMEM((1, docs), jnp.int32),
                pltpu.SemaphoreType.DMA,
                pltpu.SemaphoreType.DMA((heads,)),
                pltpu.SemaphoreType.DMA((2, 3)),
                pltpu.SemaphoreType.DMA((2, 2, heads)),
                pltpu.SemaphoreType.DMA,
                pltpu.SemaphoreType.DMA,
                pltpu.SemaphoreType.DMA,
                pltpu.SemaphoreType.REGULAR,
            ],
            compiler_params=pltpu.CompilerParams(
                collective_id=0, has_side_effects=True
            ),
        )(queries, keys, values, out_grad, doc_lengths.reshape(1, -1))
        part = jax.ShapeDtypeStruct((rows_out, width * groups), BF16)
        return pl.pallas_call(
            split,
            out_shape=(part, part, part),
            in_specs=[pl.BlockSpec(memory_space=pltpu.VMEM)],
            out_specs=(pl.BlockSpec(memory_space=pl.ANY),) * 3,
            scratch_shapes=[pltpu.SemaphoreType.DMA],
            compiler_params=pltpu.CompilerParams(vmem_limit_bytes=8 << 20),
        )(out)

    return shards


def solution(mesh):
    return jax.shard_map(
        make_shards(mesh.shape["seq"], mesh.shape["head"]),
        mesh=mesh,
        in_specs=(P("seq", "head"), P("seq", "head"), P("seq", "head"), P("seq", "head"), P()),
        out_specs=(P(("seq", "head"), None), P(("seq", "head"), None), P(("seq", "head"), None)),
        check_vma=False,
    )
```
